128 devices in a mesh: gz: 16 (over z, y), gy: 8 (over x, core).
Axes of the slice: x: 4, y: 4, z: 4, core: 2. Of those that a mesh axis runs over, the one named last changes fastest.
Arguments:
- species_field: float32 [4, 512, 512, 512], P(None, 'gz', 'gy'), may hold values from -100 to 100
Outputs:
- core_tensor: float32 [4, 512, 4096], P(None, ('gz', 'gy'))
- basis_z: float32 [512, 64], replicated
- basis_y: float32 [512, 64], replicated
The draws below stay inside these ranges and needn't reach their ends.
All inputs are finite; a program needn't handle non-finite values.
Results may differ from the reference program's by a relative error of at most 0.0003.
Values sent between devices are 32-bit elements; how exact they have to be, the bound alone decides.
A program may use at most 192 MiB of HBM per device.

```python
import math
import jax
import jax.numpy as jnp
from jax import lax

SPECIES = 4
GRID = 512
RANK = 64
ITERS = 4
NX = 512


def draw_species_field(key, part):
    key_noise, key_u, key_v, key_w, key_y, key_z = jax.random.split(key, 6)
    mode_count = 2 * RANK
    shape_all = (SPECIES, GRID, GRID, NX)
    mode_index = jnp.arange(mode_count).astype(jnp.float32)
    top_level = 8.0
    fall_off = math.log(0.1)
    noise_values = jnp.clip(jax.random.normal(key_noise, shape_all, jnp.float32), -6.0, 6.0)
    along_z = jnp.clip(jax.random.normal(key_u, (mode_count, GRID), jnp.float32), -6.0, 6.0)
    along_y = jnp.clip(jax.random.normal(key_v, (mode_count, GRID), jnp.float32), -6.0, 6.0)
    along_x = jnp.clip(jax.random.normal(key_w, (mode_count, SPECIES, NX), jnp.float32), -6.0, 6.0)
    scale_y = jnp.exp(jax.random.uniform(key_y, (GRID,), jnp.float32, 0.0, math.log(1.4)))
    scale_z = jnp.exp(jax.random.uniform(key_z, (GRID,), jnp.float32, 0.0, math.log(1.4)))
    amplitude = jnp.sqrt(top_level * jnp.exp(fall_off * mode_index / mode_count) / GRID)
    plane_modes = along_z[:, :, None] * along_y[:, None, :] * amplitude[:, None, None]
    signal_part = jnp.einsum('kzy,ksx->szyx', plane_modes, along_x, precision=lax.Precision.HIGHEST)
    field_values = (signal_part + noise_values) * scale_z[None, :, None, None] * scale_y[None, None, :, None]
    return jnp.clip(field_values, -100.0, 100.0)


def setup_inputs(seed: int = 0) -> dict:
    key_list = jax.random.split(jax.random.key(seed), 2)
    species_field = draw_species_field(jax.random.fold_in(key_list[1], 71), 0)
    return {"species_field": species_field}


def start_table(order, width):
    row_index = jnp.arange(order).astype(jnp.float32)
    col_index = jnp.arange(width).astype(jnp.float32)
    return jnp.cos(math.pi * (row_index[:, None] + 0.5) * col_index[None, :] / order)

def refine_basis(matrix, current):
    product = jnp.dot(matrix, current, precision=lax.Precision.HIGHEST)
    inner_gram = lax.dot_general(product, product, (((0,), (0,)), ((), ())), precision=lax.Precision.HIGHEST)
    factor = jnp.linalg.cholesky(inner_gram)
    return lax.linalg.triangular_solve(factor, product, left_side=False, lower=True, transpose_a=True)

def leaf_basis(gram_matrix):
    basis_now = start_table(GRID, RANK)
    for iteration in range(ITERS):
        basis_now = refine_basis(gram_matrix, basis_now)
    return basis_now

def mode_gram(fibres, mode):
    others = tuple((d for d in range(4) if d != mode))
    return lax.dot_general(fibres, fibres, ((others, others), ((), ())), precision=lax.Precision.HIGHEST)

def reference(species_field):
    gram_z = mode_gram(species_field, 1)
    basis_z = leaf_basis(gram_z)
    reduced = jnp.einsum('szyx,zr->sryx', species_field, basis_z, precision=lax.Precision.HIGHEST)
    gram_y = mode_gram(reduced, 2)
    basis_y = leaf_basis(gram_y)
    core_tensor = jnp.einsum('sryx,yq->sxrq', reduced, basis_y, precision=lax.Precision.HIGHEST)
    core_tensor = core_tensor.reshape(SPECIES, NX, RANK * RANK)
    return (core_tensor, basis_z, basis_y)
```

```python
import math

import jax
import jax.numpy as jnp
from jax import lax
from jax.sharding import PartitionSpec as P

GRID = 512
RANK = 64
ITERS = 4


def start_table(order, width):
    row_index = jnp.arange(order).astype(jnp.float32)
    col_index = jnp.arange(width).astype(jnp.float32)
    return jnp.cos(math.pi * (row_index[:, None] + 0.5) * col_index[None, :] / order)


def solve_factor(product, inner_gram):
    factor = jnp.linalg.cholesky(inner_gram)
    return lax.linalg.triangular_solve(
        factor, product, left_side=False, lower=True, transpose_a=True
    )


def inner_products(left, right):
    return lax.dot_general(left, right, (((0,), (0,)), ((), ())), precision=lax.Precision.HIGHEST)


def mode_products(left, right, mode):
    others = tuple((d for d in range(4) if d != mode))
    return lax.dot_general(
        left, right, ((others, others), ((), ())), precision=lax.Precision.HIGHEST
    )


def sum_over_mesh(gram):
    axes = ("gz", "gy")
    count = lax.axis_size("gz") * lax.axis_size("gy")
    rows = gram.shape[0]
    parts = lax.all_to_all(
        gram.reshape(count, rows // count, rows), axes, 0, 0, tiled=True
    )
    mine = parts.sum(0)
    tiled = jnp.broadcast_to(mine[None], (count,) + mine.shape)
    return lax.all_to_all(tiled, axes, 0, 0, tiled=True).reshape(rows, rows)


def leaf_basis(fibres, mode):
    basis_now = start_table(GRID, RANK)
    gram_total = sum_over_mesh(mode_products(fibres, fibres, mode))
    for iteration in range(ITERS):
        product = jnp.dot(gram_total, basis_now, precision=lax.Precision.HIGHEST)
        basis_now = solve_factor(product, inner_products(product, product))
    return basis_now


def body(species_field):
    fibres_z = lax.all_to_all(species_field, "gz", split_axis=2, concat_axis=1, tiled=True)
    basis_z = leaf_basis(fibres_z, 1)
    reduced = jnp.einsum("szyx,zr->sryx", fibres_z, basis_z, precision=lax.Precision.HIGHEST)
    mixed = lax.all_to_all(reduced, ("gz", "gy"), split_axis=3, concat_axis=2, tiled=True)
    count_gz = lax.axis_size("gz")
    count_gy = lax.axis_size("gy")
    shape_now = mixed.shape
    y_local = shape_now[2] // (count_gz * count_gy)
    blocks = mixed.reshape(shape_now[0], shape_now[1], count_gz, count_gy, y_local, shape_now[3])
    fibres_y = jnp.transpose(blocks, (0, 1, 3, 2, 4, 5)).reshape(shape_now)
    basis_y = leaf_basis(fibres_y, 2)
    core_tensor = jnp.einsum("sryx,yq->sxrq", fibres_y, basis_y, precision=lax.Precision.HIGHEST)
    core_tensor = core_tensor.reshape(fibres_y.shape[0], fibres_y.shape[3], RANK * RANK)
    return (core_tensor, basis_z, basis_y)


def solution(mesh):
    in_specs = (P(None, "gz", "gy", None),)
    out_specs = (P(None, ("gz", "gy"), None), P(), P())
    return jax.shard_map(body, mesh=mesh, in_specs=in_specs, out_specs=out_specs, check_vma=False)
```

```python
import math

import jax
import jax.numpy as jnp
from jax import lax
from jax.sharding import PartitionSpec as P

GRID = 512
RANK = 64
ITERS = 4


def start_table(order, width):
    row_index = jnp.arange(order).astype(jnp.float32)
    col_index = jnp.arange(width).astype(jnp.float32)
    return jnp.cos(math.pi * (row_index[:, None] + 0.5) * col_index[None, :] / order)


def solve_factor(product, inner_gram):
    factor = jnp.linalg.cholesky(inner_gram)
    return lax.linalg.triangular_solve(
        factor, product, left_side=False, lower=True, transpose_a=True
    )


def inner_products(left, right):
    return lax.dot_general(left, right, (((0,), (0,)), ((), ())), precision=lax.Precision.HIGHEST)


def mode_products(left, right, mode):
    others = tuple((d for d in range(4) if d != mode))
    return lax.dot_general(
        left, right, ((others, others), ((), ())), precision=lax.Precision.HIGH
    )


def sum_over_mesh(gram):
    axes = ("gz", "gy")
    count = lax.axis_size("gz") * lax.axis_size("gy")
    rows = gram.shape[0]
    parts = lax.all_to_all(
        gram.reshape(count, rows // count, rows), axes, 0, 0, tiled=True
    )
    mine = parts.sum(0)
    tiled = jnp.broadcast_to(mine[None], (count,) + mine.shape)
    return lax.all_to_all(tiled, axes, 0, 0, tiled=True).reshape(rows, rows)


def leaf_basis(fibres, mode):
    basis_now = start_table(GRID, RANK)
    gram_total = sum_over_mesh(mode_products(fibres, fibres, mode))
    for iteration in range(ITERS):
        product = jnp.dot(gram_total, basis_now, precision=lax.Precision.HIGHEST)
        basis_now = solve_factor(product, inner_products(product, product))
    return basis_now


def body(species_field):
    fibres_z = lax.all_to_all(species_field, "gz", split_axis=2, concat_axis=1, tiled=True)
    basis_z = leaf_basis(fibres_z, 1)
    reduced = jnp.einsum("szyx,zr->sryx", fibres_z, basis_z, precision=lax.Precision.HIGH)
    mixed = lax.all_to_all(reduced, ("gz", "gy"), split_axis=3, concat_axis=2, tiled=True)
    count_gz = lax.axis_size("gz")
    count_gy = lax.axis_size("gy")
    shape_now = mixed.shape
    y_local = shape_now[2] // (count_gz * count_gy)
    blocks = mixed.reshape(shape_now[0], shape_now[1], count_gz, count_gy, y_local, shape_now[3])
    fibres_y = jnp.transpose(blocks, (0, 1, 3, 2, 4, 5)).reshape(shape_now)
    basis_y = leaf_basis(fibres_y, 2)
    core_tensor = jnp.einsum("sryx,yq->sxrq", fibres_y, basis_y, precision=lax.Precision.HIGH)
    core_tensor = core_tensor.reshape(fibres_y.shape[0], fibres_y.shape[3], RANK * RANK)
    return (core_tensor, basis_z, basis_y)


def solution(mesh):
    in_specs = (P(None, "gz", "gy", None),)
    out_specs = (P(None, ("gz", "gy"), None), P(), P())
    return jax.shard_map(body, mesh=mesh, in_specs=in_specs, out_specs=out_specs, check_vma=False)
```

```python
import math

import jax
import jax.numpy as jnp
from jax import lax
from jax.experimental import pallas as pl
from jax.experimental.pallas import tpu as pltpu
from jax.sharding import PartitionSpec as P
import functools

GRID = 512
RANK = 64
ITERS = 4


def start_table(order, width):
    row_index = jnp.arange(order).astype(jnp.float32)
    col_index = jnp.arange(width).astype(jnp.float32)
    return jnp.cos(math.pi * (row_index[:, None] + 0.5) * col_index[None, :] / order)


def solve_factor(product, inner_gram):
    factor = jnp.linalg.cholesky(inner_gram)
    return lax.linalg.triangular_solve(
        factor, product, left_side=False, lower=True, transpose_a=True
    )


def inner_products(left, right):
    return lax.dot_general(left, right, (((0,), (0,)), ((), ())), precision=lax.Precision.HIGHEST)


def mode_products(left, right, mode):
    others = tuple((d for d in range(4) if d != mode))
    return lax.dot_general(
        left, right, ((others, others), ((), ())), precision=lax.Precision.HIGH
    )


def sum_over_mesh(gram):
    axes = ("gz", "gy")
    count = lax.axis_size("gz") * lax.axis_size("gy")
    rows = gram.shape[0]
    parts = lax.all_to_all(
        gram.reshape(count, rows // count, rows), axes, 0, 0, tiled=True
    )
    mine = parts.sum(0)
    tiled = jnp.broadcast_to(mine[None], (count,) + mine.shape)
    return lax.all_to_all(tiled, axes, 0, 0, tiled=True).reshape(rows, rows)


def _eliminate(c):
    n = c.shape[0]
    row = lax.broadcasted_iota(jnp.int32, (n, n), 0)
    lane = lax.broadcasted_iota(jnp.int32, (n, n), 1)
    right = (row == lane).astype(jnp.float32)

    def step(j, carry):
        left, right = carry
        at_row = row == j
        row_l = jnp.sum(jnp.where(at_row, left, 0.0), axis=0, keepdims=True)
        row_r = jnp.sum(jnp.where(at_row, right, 0.0), axis=0, keepdims=True)
        col = jnp.sum(jnp.where(lane == j, left, 0.0), axis=1, keepdims=True)
        pivot = jnp.sum(jnp.where(row[:, :1] == j, col, 0.0), axis=0, keepdims=True)
        factor = jnp.where(row[:, :1] > j, col / pivot, 0.0)
        left = left - factor * row_l
        right = right - factor * row_r
        return left, right

    left, right = lax.fori_loop(0, n, step, (c, right), unroll=8)
    diag = jnp.sum(jnp.where(row == lane, left, 0.0), axis=1, keepdims=True)
    return right / jnp.sqrt(diag)


def _basis_kernel(iters, g_ref, q_ref, out_ref):
    gram = g_ref[...]
    basis = q_ref[...]
    for _ in range(iters):
        product = jnp.dot(gram, basis, precision=lax.Precision.HIGHEST, preferred_element_type=jnp.float32)
        inner = lax.dot_general(product, product, (((0,), (0,)), ((), ())),
                                precision=lax.Precision.HIGHEST, preferred_element_type=jnp.float32)
        inverse = _eliminate(inner)
        basis = lax.dot_general(product, inverse, (((1,), (1,)), ((), ())),
                                precision=lax.Precision.HIGHEST, preferred_element_type=jnp.float32)
    out_ref[...] = basis


def basis_pallas(gram, start, iters=4):
    n, r = start.shape
    return pl.pallas_call(
        functools.partial(_basis_kernel, iters),
        out_shape=jax.ShapeDtypeStruct((n, r), jnp.float32),
        in_specs=[pl.BlockSpec(memory_space=pltpu.VMEM)] * 2,
        out_specs=pl.BlockSpec(memory_space=pltpu.VMEM),
    )(gram, start)


def leaf_basis(fibres, mode):
    basis_now = start_table(GRID, RANK)
    gram_total = sum_over_mesh(mode_products(fibres, fibres, mode))
    return basis_pallas(gram_total, basis_now, ITERS)


def body(species_field):
    fibres_z = lax.all_to_all(species_field, "gz", split_axis=2, concat_axis=1, tiled=True)
    basis_z = leaf_basis(fibres_z, 1)
    reduced = jnp.einsum("szyx,zr->sryx", fibres_z, basis_z, precision=lax.Precision.HIGH)
    mixed = lax.all_to_all(reduced, ("gz", "gy"), split_axis=3, concat_axis=2, tiled=True)
    count_gz = lax.axis_size("gz")
    count_gy = lax.axis_size("gy")
    shape_now = mixed.shape
    y_local = shape_now[2] // (count_gz * count_gy)
    blocks = mixed.reshape(shape_now[0], shape_now[1], count_gz, count_gy, y_local, shape_now[3])
    fibres_y = jnp.transpose(blocks, (0, 1, 3, 2, 4, 5)).reshape(shape_now)
    basis_y = leaf_basis(fibres_y, 2)
    core_tensor = jnp.einsum("sryx,yq->sxrq", fibres_y, basis_y, precision=lax.Precision.HIGH)
    core_tensor = core_tensor.reshape(fibres_y.shape[0], fibres_y.shape[3], RANK * RANK)
    return (core_tensor, basis_z, basis_y)


def solution(mesh):
    in_specs = (P(None, "gz", "gy", None),)
    out_specs = (P(None, ("gz", "gy"), None), P(), P())
    return jax.shard_map(body, mesh=mesh, in_specs=in_specs, out_specs=out_specs, check_vma=False)
```

```python
import math

import jax
import jax.numpy as jnp
from jax import lax
from jax.experimental import pallas as pl
from jax.experimental.pallas import tpu as pltpu
from jax.sharding import PartitionSpec as P
import functools

GRID = 512
RANK = 64
ITERS = 4
CHUNK = 1


def start_table(order, width):
    row_index = jnp.arange(order).astype(jnp.float32)
    col_index = jnp.arange(width).astype(jnp.float32)
    return jnp.cos(math.pi * (row_index[:, None] + 0.5) * col_index[None, :] / order)


def solve_factor(product, inner_gram):
    factor = jnp.linalg.cholesky(inner_gram)
    return lax.linalg.triangular_solve(
        factor, product, left_side=False, lower=True, transpose_a=True
    )


def inner_products(left, right):
    return lax.dot_general(left, right, (((0,), (0,)), ((), ())), precision=lax.Precision.HIGHEST)


def mode_products(left, right, mode):
    others = tuple((d for d in range(4) if d != mode))
    return lax.dot_general(
        left, right, ((others, others), ((), ())), precision=lax.Precision.HIGH
    )


def sum_over_mesh(gram):
    axes = ("gz", "gy")
    count = lax.axis_size("gz") * lax.axis_size("gy")
    rows = gram.shape[0]
    parts = lax.all_to_all(
        gram.reshape(count, rows // count, rows), axes, 0, 0, tiled=True
    )
    mine = parts.sum(0)
    tiled = jnp.broadcast_to(mine[None], (count,) + mine.shape)
    return lax.all_to_all(tiled, axes, 0, 0, tiled=True).reshape(rows, rows)


def _eliminate(c):
    n = c.shape[0]
    row = lax.broadcasted_iota(jnp.int32, (n, n), 0)
    lane = lax.broadcasted_iota(jnp.int32, (n, n), 1)
    right = (row == lane).astype(jnp.float32)

    def step(j, carry):
        left, right = carry
        at_row = row == j
        row_l = jnp.sum(jnp.where(at_row, left, 0.0), axis=0, keepdims=True)
        row_r = jnp.sum(jnp.where(at_row, right, 0.0), axis=0, keepdims=True)
        col = jnp.sum(jnp.where(lane == j, left, 0.0), axis=1, keepdims=True)
        pivot = jnp.sum(jnp.where(row[:, :1] == j, col, 0.0), axis=0, keepdims=True)
        factor = jnp.where(row[:, :1] > j, col / pivot, 0.0)
        left = left - factor * row_l
        right = right - factor * row_r
        return left, right

    left, right = lax.fori_loop(0, n, step, (c, right), unroll=8)
    diag = jnp.sum(jnp.where(row == lane, left, 0.0), axis=1, keepdims=True)
    return right / jnp.sqrt(diag)


def _basis_kernel(iters, g_ref, q_ref, out_ref):
    gram = g_ref[...]
    basis = q_ref[...]
    for _ in range(iters):
        product = jnp.dot(gram, basis, precision=lax.Precision.HIGHEST, preferred_element_type=jnp.float32)
        inner = lax.dot_general(product, product, (((0,), (0,)), ((), ())),
                                precision=lax.Precision.HIGHEST, preferred_element_type=jnp.float32)
        inverse = _eliminate(inner)
        basis = lax.dot_general(product, inverse, (((1,), (1,)), ((), ())),
                                precision=lax.Precision.HIGHEST, preferred_element_type=jnp.float32)
    out_ref[...] = basis


def basis_pallas(gram, start, iters=4):
    n, r = start.shape
    return pl.pallas_call(
        functools.partial(_basis_kernel, iters),
        out_shape=jax.ShapeDtypeStruct((n, r), jnp.float32),
        in_specs=[pl.BlockSpec(memory_space=pltpu.VMEM)] * 2,
        out_specs=pl.BlockSpec(memory_space=pltpu.VMEM),
    )(gram, start)


def leaf_basis(gram_part):
    basis_now = start_table(GRID, RANK)
    gram_total = sum_over_mesh(gram_part)
    return basis_pallas(gram_total, basis_now, ITERS)


def body(species_field):
    pieces = species_field.shape[0] // CHUNK
    fibres = [
        lax.all_to_all(
            species_field[CHUNK * k : CHUNK * (k + 1)], "gz", split_axis=2, concat_axis=1, tiled=True
        )
        for k in range(pieces)
    ]
    gram_z = mode_products(fibres[0], fibres[0], 1)
    for part in fibres[1:]:
        gram_z = gram_z + mode_products(part, part, 1)
    basis_z = leaf_basis(gram_z)
    reduced = jnp.concatenate(
        [
            jnp.einsum("szyx,zr->sryx", part, basis_z, precision=lax.Precision.HIGH)
            for part in fibres
        ],
        axis=0,
    )
    mixed = lax.all_to_all(reduced, ("gz", "gy"), split_axis=3, concat_axis=2, tiled=True)
    count_gz = lax.axis_size("gz")
    count_gy = lax.axis_size("gy")
    shape_now = mixed.shape
    y_local = shape_now[2] // (count_gz * count_gy)
    blocks = mixed.reshape(shape_now[0], shape_now[1], count_gz, count_gy, y_local, shape_now[3])
    fibres_y = jnp.transpose(blocks, (0, 1, 3, 2, 4, 5)).reshape(shape_now)
    basis_y = leaf_basis(mode_products(fibres_y, fibres_y, 2))
    core_tensor = jnp.einsum("sryx,yq->sxrq", fibres_y, basis_y, precision=lax.Precision.HIGH)
    core_tensor = core_tensor.reshape(fibres_y.shape[0], fibres_y.shape[3], RANK * RANK)
    return (core_tensor, basis_z, basis_y)


def solution(mesh):
    in_specs = (P(None, "gz", "gy", None),)
    out_specs = (P(None, ("gz", "gy"), None), P(), P())
    return jax.shard_map(body, mesh=mesh, in_specs=in_specs, out_specs=out_specs, check_vma=False)
```

```python
import math

import jax
import jax.numpy as jnp
from jax import lax
from jax.experimental import pallas as pl
from jax.experimental.pallas import tpu as pltpu
from jax.sharding import PartitionSpec as P
import functools

GRID = 512
RANK = 64
ITERS = 4
CHUNK = 4


def start_table(order, width):
    row_index = jnp.arange(order).astype(jnp.float32)
    col_index = jnp.arange(width).astype(jnp.float32)
    return jnp.cos(math.pi * (row_index[:, None] + 0.5) * col_index[None, :] / order)


def solve_factor(product, inner_gram):
    factor = jnp.linalg.cholesky(inner_gram)
    return lax.linalg.triangular_solve(
        factor, product, left_side=False, lower=True, transpose_a=True
    )


def inner_products(left, right):
    return lax.dot_general(left, right, (((0,), (0,)), ((), ())), precision=lax.Precision.HIGHEST)


def mode_products(left, right, mode):
    others = tuple((d for d in range(4) if d != mode))
    return lax.dot_general(
        left, right, ((others, others), ((), ())), precision=lax.Precision.HIGH
    )


def sum_over_mesh(gram):
    axes = ("gz", "gy")
    count = lax.axis_size("gz") * lax.axis_size("gy")
    rows = gram.shape[0]
    parts = lax.all_to_all(
        gram.reshape(count, rows // count, rows), axes, 0, 0, tiled=True
    )
    mine = parts.sum(0)
    tiled = jnp.broadcast_to(mine[None], (count,) + mine.shape)
    return lax.all_to_all(tiled, axes, 0, 0, tiled=True).reshape(rows, rows)


def _eliminate(c):
    n = c.shape[0]
    row = lax.broadcasted_iota(jnp.int32, (n, n), 0)
    lane = lax.broadcasted_iota(jnp.int32, (n, n), 1)
    right = (row == lane).astype(jnp.float32)

    def step(j, carry):
        left, right = carry
        at_row = row == j
        row_l = jnp.sum(jnp.where(at_row, left, 0.0), axis=0, keepdims=True)
        row_r = jnp.sum(jnp.where(at_row, right, 0.0), axis=0, keepdims=True)
        col = jnp.sum(jnp.where(lane == j, left, 0.0), axis=1, keepdims=True)
        pivot = jnp.sum(jnp.where(row[:, :1] == j, col, 0.0), axis=0, keepdims=True)
        factor = jnp.where(row[:, :1] > j, col / pivot, 0.0)
        left = left - factor * row_l
        right = right - factor * row_r
        return left, right

    left, right = lax.fori_loop(0, n, step, (c, right), unroll=8)
    diag = jnp.sum(jnp.where(row == lane, left, 0.0), axis=1, keepdims=True)
    return right / jnp.sqrt(diag)


def _basis_kernel(iters, g_ref, q_ref, out_ref):
    gram = g_ref[...]
    basis = q_ref[...]
    for _ in range(iters):
        product = jnp.dot(gram, basis, precision=lax.Precision.HIGHEST, preferred_element_type=jnp.float32)
        inner = lax.dot_general(product, product, (((0,), (0,)), ((), ())),
                                precision=lax.Precision.HIGHEST, preferred_element_type=jnp.float32)
        inverse = _eliminate(inner)
        basis = lax.dot_general(product, inverse, (((1,), (1,)), ((), ())),
                                precision=lax.Precision.HIGHEST, preferred_element_type=jnp.float32)
    out_ref[...] = basis


def basis_pallas(gram, start, iters=4):
    n, r = start.shape
    return pl.pallas_call(
        functools.partial(_basis_kernel, iters),
        out_shape=jax.ShapeDtypeStruct((n, r), jnp.float32),
        in_specs=[pl.BlockSpec(memory_space=pltpu.VMEM)] * 2,
        out_specs=pl.BlockSpec(memory_space=pltpu.VMEM),
    )(gram, start)


def leaf_basis(gram_part):
    basis_now = start_table(GRID, RANK)
    gram_total = sum_over_mesh(gram_part)
    return basis_pallas(gram_total, basis_now, ITERS)


def body(species_field):
    pieces = species_field.shape[0] // CHUNK
    fibres = [
        lax.all_to_all(
            species_field[CHUNK * k : CHUNK * (k + 1)], "gz", split_axis=2, concat_axis=1, tiled=True
        )
        for k in range(pieces)
    ]
    gram_z = None
    for part in fibres:
        for one in range(part.shape[0]):
            term = mode_products(part[one : one + 1], part[one : one + 1], 1)
            gram_z = term if gram_z is None else gram_z + term
    basis_z = leaf_basis(gram_z)
    reduced = jnp.concatenate(
        [
            jnp.einsum("szyx,zr->sryx", part, basis_z, precision=lax.Precision.HIGH)
            for part in fibres
        ],
        axis=0,
    )
    mixed = lax.all_to_all(reduced, ("gz", "gy"), split_axis=3, concat_axis=2, tiled=True)
    count_gz = lax.axis_size("gz")
    count_gy = lax.axis_size("gy")
    shape_now = mixed.shape
    y_local = shape_now[2] // (count_gz * count_gy)
    blocks = mixed.reshape(shape_now[0], shape_now[1], count_gz, count_gy, y_local, shape_now[3])
    fibres_y = jnp.transpose(blocks, (0, 1, 3, 2, 4, 5)).reshape(shape_now)
    basis_y = leaf_basis(mode_products(fibres_y, fibres_y, 2))
    core_tensor = jnp.einsum("sryx,yq->sxrq", fibres_y, basis_y, precision=lax.Precision.HIGH)
    core_tensor = core_tensor.reshape(fibres_y.shape[0], fibres_y.shape[3], RANK * RANK)
    return (core_tensor, basis_z, basis_y)


def solution(mesh):
    in_specs = (P(None, "gz", "gy", None),)
    out_specs = (P(None, ("gz", "gy"), None), P(), P())
    return jax.shard_map(body, mesh=mesh, in_specs=in_specs, out_specs=out_specs, check_vma=False)
```

```python
import math

import jax
import jax.numpy as jnp
from jax import lax
from jax.experimental import pallas as pl
from jax.experimental.pallas import tpu as pltpu
from jax.sharding import PartitionSpec as P
import functools

GRID = 512
RANK = 64
ITERS = 4


def start_table(order, width):
    row_index = jnp.arange(order).astype(jnp.float32)
    col_index = jnp.arange(width).astype(jnp.float32)
    return jnp.cos(math.pi * (row_index[:, None] + 0.5) * col_index[None, :] / order)


def solve_factor(product, inner_gram):
    factor = jnp.linalg.cholesky(inner_gram)
    return lax.linalg.triangular_solve(
        factor, product, left_side=False, lower=True, transpose_a=True
    )


def inner_products(left, right):
    return lax.dot_general(left, right, (((0,), (0,)), ((), ())), precision=lax.Precision.HIGHEST)


def mode_products(left, right, mode):
    others = tuple((d for d in range(4) if d != mode))
    return lax.dot_general(
        left, right, ((others, others), ((), ())), precision=lax.Precision.HIGH
    )


def sum_over_mesh(gram):
    axes = ("gz", "gy")
    count = lax.axis_size("gz") * lax.axis_size("gy")
    rows = gram.shape[0]
    parts = lax.all_to_all(
        gram.reshape(count, rows // count, rows), axes, 0, 0, tiled=True
    )
    mine = parts.sum(0)
    tiled = jnp.broadcast_to(mine[None], (count,) + mine.shape)
    return lax.all_to_all(tiled, axes, 0, 0, tiled=True).reshape(rows, rows)


def _eliminate(c):
    n = c.shape[0]
    row = lax.broadcasted_iota(jnp.int32, (n, n), 0)
    lane = lax.broadcasted_iota(jnp.int32, (n, n), 1)
    right = (row == lane).astype(jnp.float32)

    def step(j, carry):
        left, right = carry
        at_row = row == j
        row_l = jnp.sum(jnp.where(at_row, left, 0.0), axis=0, keepdims=True)
        row_r = jnp.sum(jnp.where(at_row, right, 0.0), axis=0, keepdims=True)
        col = jnp.sum(jnp.where(lane == j, left, 0.0), axis=1, keepdims=True)
        pivot = jnp.sum(jnp.where(row[:, :1] == j, col, 0.0), axis=0, keepdims=True)
        factor = jnp.where(row[:, :1] > j, col / pivot, 0.0)
        left = left - factor * row_l
        right = right - factor * row_r
        return left, right

    left, right = lax.fori_loop(0, n, step, (c, right), unroll=8)
    diag = jnp.sum(jnp.where(row == lane, left, 0.0), axis=1, keepdims=True)
    return right / jnp.sqrt(diag)


def _basis_kernel(iters, g_ref, q_ref, out_ref):
    gram = g_ref[...]
    basis = q_ref[...]
    for _ in range(iters):
        product = jnp.dot(gram, basis, precision=lax.Precision.HIGHEST, preferred_element_type=jnp.float32)
        inner = lax.dot_general(product, product, (((0,), (0,)), ((), ())),
                                precision=lax.Precision.HIGHEST, preferred_element_type=jnp.float32)
        inverse = _eliminate(inner)
        basis = lax.dot_general(product, inverse, (((1,), (1,)), ((), ())),
                                precision=lax.Precision.HIGHEST, preferred_element_type=jnp.float32)
    out_ref[...] = basis


def basis_pallas(gram, start, iters=4):
    n, r = start.shape
    return pl.pallas_call(
        functools.partial(_basis_kernel, iters),
        out_shape=jax.ShapeDtypeStruct((n, r), jnp.float32),
        in_specs=[pl.BlockSpec(memory_space=pltpu.VMEM)] * 2,
        out_specs=pl.BlockSpec(memory_space=pltpu.VMEM),
    )(gram, start)


def leaf_basis(gram_part, basis_now):
    gram_total = sum_over_mesh(gram_part)
    return basis_pallas(gram_total, basis_now, ITERS)


def body(species_field):
    count_gz = lax.axis_size("gz")
    count_gy = lax.axis_size("gy")
    count = count_gz * count_gy
    fibres = lax.all_to_all(species_field, "gz", split_axis=2, concat_axis=1, tiled=True)
    species, _, y_local, x_size = fibres.shape
    gram_z = None
    for one in range(species):
        term = mode_products(fibres[one : one + 1], fibres[one : one + 1], 1)
        gram_z = term if gram_z is None else gram_z + term
    basis_z = leaf_basis(gram_z, start_table(GRID, RANK))
    reduced = jnp.einsum("szyx,zr->xysr", fibres, basis_z, precision=lax.Precision.HIGH)
    x_part = x_size // count
    send = reduced.reshape(count, x_part, y_local, species, RANK)
    send = jnp.transpose(send, (0, 2, 1, 3, 4)).reshape(count, -1)
    mixed = lax.all_to_all(send, ("gz", "gy"), 0, 0, tiled=True)
    fibres_y = mixed.reshape(count, y_local, -1)
    fibres_y = jnp.transpose(fibres_y, (1, 0, 2)).reshape(count * y_local, -1)
    gram_y = lax.dot_general(
        fibres_y, fibres_y, (((1,), (1,)), ((), ())), precision=lax.Precision.HIGH
    )
    start_y = start_table(GRID, RANK).reshape(count_gy, count_gz, y_local, RANK)
    start_y = jnp.transpose(start_y, (2, 1, 0, 3)).reshape(GRID, RANK)
    basis_perm = leaf_basis(gram_y, start_y)
    core_rows = lax.dot_general(
        fibres_y, basis_perm, (((0,), (0,)), ((), ())), precision=lax.Precision.HIGH
    )
    core_tensor = core_rows.reshape(x_part, species, RANK, RANK)
    core_tensor = jnp.transpose(core_tensor, (1, 0, 2, 3)).reshape(species, x_part, RANK * RANK)
    basis_y = basis_perm.reshape(y_local, count_gz, count_gy, RANK)
    basis_y = jnp.transpose(basis_y, (2, 1, 0, 3)).reshape(GRID, RANK)
    return (core_tensor, basis_z, basis_y)


def solution(mesh):
    in_specs = (P(None, "gz", "gy", None),)
    out_specs = (P(None, ("gz", "gy"), None), P(), P())
    return jax.shard_map(body, mesh=mesh, in_specs=in_specs, out_specs=out_specs, check_vma=False)
```

```python
import math

import jax
import jax.numpy as jnp
from jax import lax
from jax.experimental import pallas as pl
from jax.experimental.pallas import tpu as pltpu
from jax.sharding import PartitionSpec as P
import functools

GRID = 512
RANK = 64
ITERS = 4


def start_table(order, width):
    row_index = jnp.arange(order).astype(jnp.float32)
    col_index = jnp.arange(width).astype(jnp.float32)
    return jnp.cos(math.pi * (row_index[:, None] + 0.5) * col_index[None, :] / order)


def solve_factor(product, inner_gram):
    factor = jnp.linalg.cholesky(inner_gram)
    return lax.linalg.triangular_solve(
        factor, product, left_side=False, lower=True, transpose_a=True
    )


def inner_products(left, right):
    return lax.dot_general(left, right, (((0,), (0,)), ((), ())), precision=lax.Precision.HIGHEST)


def mode_products(left, right, mode):
    others = tuple((d for d in range(4) if d != mode))
    return lax.dot_general(
        left, right, ((others, others), ((), ())), precision=lax.Precision.HIGH
    )


def sum_over_mesh(gram):
    axes = ("gz", "gy")
    count = lax.axis_size("gz") * lax.axis_size("gy")
    rows = gram.shape[0]
    parts = lax.all_to_all(
        gram.reshape(count, rows // count, rows), axes, 0, 0, tiled=True
    )
    mine = parts.sum(0)
    tiled = jnp.broadcast_to(mine[None], (count,) + mine.shape)
    return lax.all_to_all(tiled, axes, 0, 0, tiled=True).reshape(rows, rows)


def _eliminate(c):
    n = c.shape[0]
    row = lax.broadcasted_iota(jnp.int32, (n, n), 0)
    lane = lax.broadcasted_iota(jnp.int32, (n, n), 1)
    row_col = row[:, :1]
    right = jnp.where(row == lane, 1.0, 0.0)
    diag = jnp.sum(jnp.where(row == lane, c, 0.0), axis=1, keepdims=True)

    def step(j, carry):
        left, right, diag = carry
        at_row = row == j
        row_l = jnp.sum(jnp.where(at_row, left, 0.0), axis=0, keepdims=True)
        row_r = jnp.sum(jnp.where(at_row, right, 0.0), axis=0, keepdims=True)
        col = jnp.sum(jnp.where(lane == j, left, 0.0), axis=1, keepdims=True)
        pivot = jnp.sum(jnp.where(row_col == j, diag, 0.0), axis=0, keepdims=True)
        factor = jnp.where(row_col > j, col / pivot, 0.0)
        return (left - factor * row_l, right - factor * row_r, diag - factor * col)

    _, right, diag = lax.fori_loop(0, n, step, (c, right, diag), unroll=8)
    return right / jnp.sqrt(diag)


def _basis_kernel(iters, g_ref, q_ref, out_ref):
    gram = g_ref[...]
    basis_t = q_ref[...]
    for _ in range(iters):
        product_t = jnp.dot(basis_t, gram, precision=lax.Precision.HIGHEST, preferred_element_type=jnp.float32)
        inner = lax.dot_general(product_t, product_t, (((1,), (1,)), ((), ())),
                                precision=lax.Precision.HIGHEST, preferred_element_type=jnp.float32)
        basis_t = jnp.dot(_eliminate(inner), product_t, precision=lax.Precision.HIGHEST,
                          preferred_element_type=jnp.float32)
    out_ref[...] = basis_t


def basis_pallas(gram, start, iters=4):
    size, n = start.shape
    out = pl.pallas_call(
        functools.partial(_basis_kernel, iters),
        out_shape=jax.ShapeDtypeStruct((n, size), jnp.float32),
        in_specs=[pl.BlockSpec(memory_space=pltpu.VMEM)] * 2,
        out_specs=pl.BlockSpec(memory_space=pltpu.VMEM),
    )(gram, start.T)
    return out.T

def leaf_basis(gram_part, basis_now):
    gram_total = sum_over_mesh(gram_part)
    return basis_pallas(gram_total, basis_now, ITERS)


def body(species_field):
    count_gz = lax.axis_size("gz")
    count_gy = lax.axis_size("gy")
    count = count_gz * count_gy
    fibres = lax.all_to_all(species_field, "gz", split_axis=2, concat_axis=1, tiled=True)
    species, _, y_local, x_size = fibres.shape
    gram_z = None
    for one in range(species):
        term = mode_products(fibres[one : one + 1], fibres[one : one + 1], 1)
        gram_z = term if gram_z is None else gram_z + term
    basis_z = leaf_basis(gram_z, start_table(GRID, RANK))
    reduced = jnp.einsum("szyx,zr->xysr", fibres, basis_z, precision=lax.Precision.HIGH)
    x_part = x_size // count
    send = reduced.reshape(count, x_part, y_local, species, RANK)
    send = jnp.transpose(send, (0, 2, 1, 3, 4)).reshape(count, -1)
    mixed = lax.all_to_all(send, ("gz", "gy"), 0, 0, tiled=True)
    fibres_y = mixed.reshape(count, y_local, -1)
    fibres_y = jnp.transpose(fibres_y, (1, 0, 2)).reshape(count * y_local, -1)
    gram_y = lax.dot_general(
        fibres_y, fibres_y, (((1,), (1,)), ((), ())), precision=lax.Precision.HIGH
    )
    start_y = start_table(GRID, RANK).reshape(count_gy, count_gz, y_local, RANK)
    start_y = jnp.transpose(start_y, (2, 1, 0, 3)).reshape(GRID, RANK)
    basis_perm = leaf_basis(gram_y, start_y)
    core_rows = lax.dot_general(
        fibres_y, basis_perm, (((0,), (0,)), ((), ())), precision=lax.Precision.HIGH
    )
    core_tensor = core_rows.reshape(x_part, species, RANK, RANK)
    core_tensor = jnp.transpose(core_tensor, (1, 0, 2, 3)).reshape(species, x_part, RANK * RANK)
    basis_y = basis_perm.reshape(y_local, count_gz, count_gy, RANK)
    basis_y = jnp.transpose(basis_y, (2, 1, 0, 3)).reshape(GRID, RANK)
    return (core_tensor, basis_z, basis_y)


def solution(mesh):
    in_specs = (P(None, "gz", "gy", None),)
    out_specs = (P(None, ("gz", "gy"), None), P(), P())
    return jax.shard_map(body, mesh=mesh, in_specs=in_specs, out_specs=out_specs, check_vma=False)
```

```python
import math

import jax
import jax.numpy as jnp
from jax import lax
from jax.experimental import pallas as pl
from jax.experimental.pallas import tpu as pltpu
from jax.sharding import PartitionSpec as P
import functools

GRID = 512
RANK = 64
ITERS = 4


def start_table(order, width):
    row_index = jnp.arange(order).astype(jnp.float32)
    col_index = jnp.arange(width).astype(jnp.float32)
    return jnp.cos(math.pi * (row_index[:, None] + 0.5) * col_index[None, :] / order)


def solve_factor(product, inner_gram):
    factor = jnp.linalg.cholesky(inner_gram)
    return lax.linalg.triangular_solve(
        factor, product, left_side=False, lower=True, transpose_a=True
    )


def inner_products(left, right):
    return lax.dot_general(left, right, (((0,), (0,)), ((), ())), precision=lax.Precision.HIGHEST)


def mode_products(left, right, mode):
    others = tuple((d for d in range(4) if d != mode))
    return lax.dot_general(
        left, right, ((others, others), ((), ())), precision=lax.Precision.HIGH
    )


def sum_over_mesh(gram):
    axes = ("gz", "gy")
    count = lax.axis_size("gz") * lax.axis_size("gy")
    rows = gram.shape[0]
    parts = lax.all_to_all(
        gram.reshape(count, rows // count, rows), axes, 0, 0, tiled=True
    )
    mine = parts.sum(0)
    tiled = jnp.broadcast_to(mine[None], (count,) + mine.shape)
    return lax.all_to_all(tiled, axes, 0, 0, tiled=True).reshape(rows, rows)


def _eliminate(c):
    n = c.shape[0]
    row = lax.broadcasted_iota(jnp.int32, (n, n), 0)
    lane = lax.broadcasted_iota(jnp.int32, (n, n), 1)
    row_col = row[:, :1]
    right = jnp.where(row == lane, 1.0, 0.0)
    diag = jnp.sum(jnp.where(row == lane, c, 0.0), axis=1, keepdims=True)

    def step(j, carry):
        left, right, diag = carry
        at_row = row == j
        row_l = jnp.sum(jnp.where(at_row, left, 0.0), axis=0, keepdims=True)
        row_r = jnp.sum(jnp.where(at_row, right, 0.0), axis=0, keepdims=True)
        col = jnp.sum(jnp.where(lane == j, left, 0.0), axis=1, keepdims=True)
        pivot = jnp.sum(jnp.where(row_col == j, diag, 0.0), axis=0, keepdims=True)
        factor = jnp.where(row_col > j, col / pivot, 0.0)
        return (left - factor * row_l, right - factor * row_r, diag - factor * col)

    _, right, diag = lax.fori_loop(0, n, step, (c, right, diag), unroll=8)
    return right / jnp.sqrt(diag)


def _basis_kernel(iters, g_ref, q_ref, out_ref):
    gram = g_ref[...]
    basis_t = q_ref[...]
    for _ in range(iters):
        product_t = jnp.dot(basis_t, gram, precision=lax.Precision.HIGHEST, preferred_element_type=jnp.float32)
        inner = lax.dot_general(product_t, product_t, (((1,), (1,)), ((), ())),
                                precision=lax.Precision.HIGHEST, preferred_element_type=jnp.float32)
        basis_t = jnp.dot(_eliminate(inner), product_t, precision=lax.Precision.HIGHEST,
                          preferred_element_type=jnp.float32)
    out_ref[...] = basis_t


def basis_pallas(gram, start, iters=4):
    size, n = start.shape
    out = pl.pallas_call(
        functools.partial(_basis_kernel, iters),
        out_shape=jax.ShapeDtypeStruct((n, size), jnp.float32),
        in_specs=[pl.BlockSpec(memory_space=pltpu.VMEM)] * 2,
        out_specs=pl.BlockSpec(memory_space=pltpu.VMEM),
    )(gram, start.T)
    return out.T

def _reduce_kernel(count, x_part, rank, fib_ref, bz_ref, out_ref, t_ref):
    y = pl.program_id(0)
    species = fib_ref.shape[1]
    per = 128 // rank
    for s in range(species):
        t_ref[s // per, :, (s % per) * rank : (s % per + 1) * rank] = jnp.dot(
            bz_ref[...], fib_ref[0, s],
            precision=lax.Precision.HIGH, preferred_element_type=jnp.float32).T
    width = species * rank
    for xl in range(x_part):
        for h in range(species // per):
            rows = t_ref[h, pl.ds(xl, count, stride=x_part), :]
            col = pl.multiple_of((y * x_part + xl) * width + h * 128, 128)
            out_ref[:, 0, pl.ds(col, 128)] = rows


def reduce_send(fib_ys, basis_z, count):
    ys, species, zs, xs = fib_ys.shape
    rank = basis_z.shape[1]
    x_part = xs // count
    return pl.pallas_call(
        functools.partial(_reduce_kernel, count, x_part, rank),
        grid=(ys,),
        in_specs=[pl.BlockSpec((1, species, zs, xs), lambda y: (y, 0, 0, 0)),
                  pl.BlockSpec((rank, zs), lambda y: (0, 0))],
        out_specs=pl.BlockSpec((count, 1, ys * x_part * species * rank), lambda y: (0, 0, 0)),
        out_shape=jax.ShapeDtypeStruct((count, 1, ys * x_part * species * rank), jnp.float32),
        scratch_shapes=[pltpu.VMEM((species * rank // 128, xs, 128), jnp.float32)],
        compiler_params=pltpu.CompilerParams(vmem_limit_bytes=48 * 1024 * 1024),
    )(fib_ys, basis_z.T)


def leaf_basis(gram_part, basis_now):
    gram_total = sum_over_mesh(gram_part)
    return basis_pallas(gram_total, basis_now, ITERS)


def body(species_field):
    count_gz = lax.axis_size("gz")
    count_gy = lax.axis_size("gy")
    count = count_gz * count_gy
    fibres = lax.all_to_all(species_field, "gz", split_axis=2, concat_axis=1, tiled=True)
    species, _, y_local, x_size = fibres.shape
    gram_z = None
    for one in range(species):
        term = mode_products(fibres[one : one + 1], fibres[one : one + 1], 1)
        gram_z = term if gram_z is None else gram_z + term
    basis_z = leaf_basis(gram_z, start_table(GRID, RANK))
    x_part = x_size // count
    send = reduce_send(jnp.transpose(fibres, (2, 0, 1, 3)), basis_z, count)
    mixed = lax.all_to_all(send, ("gz", "gy"), 0, 0, tiled=True)
    fibres_y = mixed.reshape(count, y_local, -1)
    fibres_y = jnp.transpose(fibres_y, (1, 0, 2)).reshape(count * y_local, -1)
    gram_y = lax.dot_general(
        fibres_y, fibres_y, (((1,), (1,)), ((), ())), precision=lax.Precision.HIGH
    )
    start_y = start_table(GRID, RANK).reshape(count_gy, count_gz, y_local, RANK)
    start_y = jnp.transpose(start_y, (2, 1, 0, 3)).reshape(GRID, RANK)
    basis_perm = leaf_basis(gram_y, start_y)
    core_rows = lax.dot_general(
        fibres_y, basis_perm, (((0,), (0,)), ((), ())), precision=lax.Precision.HIGH
    )
    core_tensor = core_rows.reshape(x_part, species, RANK, RANK)
    core_tensor = jnp.transpose(core_tensor, (1, 0, 2, 3)).reshape(species, x_part, RANK * RANK)
    basis_y = basis_perm.reshape(y_local, count_gz, count_gy, RANK)
    basis_y = jnp.transpose(basis_y, (2, 1, 0, 3)).reshape(GRID, RANK)
    return (core_tensor, basis_z, basis_y)


def solution(mesh):
    in_specs = (P(None, "gz", "gy", None),)
    out_specs = (P(None, ("gz", "gy"), None), P(), P())
    return jax.shard_map(body, mesh=mesh, in_specs=in_specs, out_specs=out_specs, check_vma=False)
```

```python
import math

import jax
import jax.numpy as jnp
from jax import lax
from jax.experimental import pallas as pl
from jax.experimental.pallas import tpu as pltpu
from jax.sharding import PartitionSpec as P
import functools

GRID = 512
RANK = 64
ITERS = 4


def start_table(order, width):
    row_index = jnp.arange(order).astype(jnp.float32)
    col_index = jnp.arange(width).astype(jnp.float32)
    return jnp.cos(math.pi * (row_index[:, None] + 0.5) * col_index[None, :] / order)


def solve_factor(product, inner_gram):
    factor = jnp.linalg.cholesky(inner_gram)
    return lax.linalg.triangular_solve(
        factor, product, left_side=False, lower=True, transpose_a=True
    )


def inner_products(left, right):
    return lax.dot_general(left, right, (((0,), (0,)), ((), ())), precision=lax.Precision.HIGHEST)


def mode_products(left, right, mode):
    others = tuple((d for d in range(4) if d != mode))
    return lax.dot_general(
        left, right, ((others, others), ((), ())), precision=lax.Precision.HIGH
    )


def sum_over_mesh(gram):
    axes = ("gz", "gy")
    count = lax.axis_size("gz") * lax.axis_size("gy")
    rows = gram.shape[0]
    parts = lax.all_to_all(
        gram.reshape(count, rows // count, rows), axes, 0, 0, tiled=True
    )
    mine = parts.sum(0)
    tiled = jnp.broadcast_to(mine[None], (count,) + mine.shape)
    return lax.all_to_all(tiled, axes, 0, 0, tiled=True).reshape(rows, rows)


def _eliminate(c):
    n = c.shape[0]
    row = lax.broadcasted_iota(jnp.int32, (n, n), 0)
    lane = lax.broadcasted_iota(jnp.int32, (n, n), 1)
    row_col = row[:, :1]
    right = jnp.where(row == lane, 1.0, 0.0)
    diag = jnp.sum(jnp.where(row == lane, c, 0.0), axis=1, keepdims=True)

    def step(j, carry):
        left, right, diag = carry
        at_row = row == j
        row_l = jnp.sum(jnp.where(at_row, left, 0.0), axis=0, keepdims=True)
        row_r = jnp.sum(jnp.where(at_row, right, 0.0), axis=0, keepdims=True)
        col = jnp.sum(jnp.where(lane == j, left, 0.0), axis=1, keepdims=True)
        pivot = jnp.sum(jnp.where(row_col == j, diag, 0.0), axis=0, keepdims=True)
        factor = jnp.where(row_col > j, col / pivot, 0.0)
        return (left - factor * row_l, right - factor * row_r, diag - factor * col)

    _, right, diag = lax.fori_loop(0, n, step, (c, right, diag), unroll=64)
    return right / jnp.sqrt(diag)


def _basis_kernel(iters, g_ref, q_ref, out_ref):
    gram = g_ref[...]
    basis_t = q_ref[...]
    for _ in range(iters):
        product_t = jnp.dot(basis_t, gram, precision=lax.Precision.HIGHEST, preferred_element_type=jnp.float32)
        inner = lax.dot_general(product_t, product_t, (((1,), (1,)), ((), ())),
                                precision=lax.Precision.HIGHEST, preferred_element_type=jnp.float32)
        basis_t = jnp.dot(_eliminate(inner), product_t, precision=lax.Precision.HIGHEST,
                          preferred_element_type=jnp.float32)
    out_ref[...] = basis_t


def basis_pallas(gram, start, iters=4):
    size, n = start.shape
    out = pl.pallas_call(
        functools.partial(_basis_kernel, iters),
        out_shape=jax.ShapeDtypeStruct((n, size), jnp.float32),
        in_specs=[pl.BlockSpec(memory_space=pltpu.VMEM)] * 2,
        out_specs=pl.BlockSpec(memory_space=pltpu.VMEM),
    )(gram, start.T)
    return out.T

def _reduce_kernel(count, x_part, rank, fib_ref, bz_ref, out_ref, t_ref):
    y = pl.program_id(0)
    species = fib_ref.shape[1]
    per = 128 // rank
    for s in range(species):
        t_ref[s // per, :, (s % per) * rank : (s % per + 1) * rank] = jnp.dot(
            bz_ref[...], fib_ref[0, s],
            precision=lax.Precision.HIGH, preferred_element_type=jnp.float32).T
    width = species * rank
    for xl in range(x_part):
        for h in range(species // per):
            rows = t_ref[h, pl.ds(xl, count, stride=x_part), :]
            col = pl.multiple_of((y * x_part + xl) * width + h * 128, 128)
            out_ref[:, 0, pl.ds(col, 128)] = rows


def reduce_send(fib_ys, basis_z, count):
    ys, species, zs, xs = fib_ys.shape
    rank = basis_z.shape[1]
    x_part = xs // count
    return pl.pallas_call(
        functools.partial(_reduce_kernel, count, x_part, rank),
        grid=(ys,),
        in_specs=[pl.BlockSpec((1, species, zs, xs), lambda y: (y, 0, 0, 0)),
                  pl.BlockSpec((rank, zs), lambda y: (0, 0))],
        out_specs=pl.BlockSpec((count, 1, ys * x_part * species * rank), lambda y: (0, 0, 0)),
        out_shape=jax.ShapeDtypeStruct((count, 1, ys * x_part * species * rank), jnp.float32),
        scratch_shapes=[pltpu.VMEM((species * rank // 128, xs, 128), jnp.float32)],
        compiler_params=pltpu.CompilerParams(vmem_limit_bytes=48 * 1024 * 1024),
    )(fib_ys, basis_z.T)


def leaf_basis(gram_part, basis_now):
    gram_total = sum_over_mesh(gram_part)
    return basis_pallas(gram_total, basis_now, ITERS)


def body(species_field):
    count_gz = lax.axis_size("gz")
    count_gy = lax.axis_size("gy")
    count = count_gz * count_gy
    fibres = lax.all_to_all(species_field, "gz", split_axis=2, concat_axis=1, tiled=True)
    species, _, y_local, x_size = fibres.shape
    gram_z = None
    for one in range(species):
        term = mode_products(fibres[one : one + 1], fibres[one : one + 1], 1)
        gram_z = term if gram_z is None else gram_z + term
    basis_z = leaf_basis(gram_z, start_table(GRID, RANK))
    x_part = x_size // count
    send = reduce_send(jnp.transpose(fibres, (2, 0, 1, 3)), basis_z, count)
    mixed = lax.all_to_all(send, ("gz", "gy"), 0, 0, tiled=True)
    fibres_y = mixed.reshape(count, y_local, -1)
    fibres_y = jnp.transpose(fibres_y, (1, 0, 2)).reshape(count * y_local, -1)
    gram_y = lax.dot_general(
        fibres_y, fibres_y, (((1,), (1,)), ((), ())), precision=lax.Precision.HIGH
    )
    start_y = start_table(GRID, RANK).reshape(count_gy, count_gz, y_local, RANK)
    start_y = jnp.transpose(start_y, (2, 1, 0, 3)).reshape(GRID, RANK)
    basis_perm = leaf_basis(gram_y, start_y)
    core_rows = lax.dot_general(
        fibres_y, basis_perm, (((0,), (0,)), ((), ())), precision=lax.Precision.HIGH
    )
    core_tensor = core_rows.reshape(x_part, species, RANK, RANK)
    core_tensor = jnp.transpose(core_tensor, (1, 0, 2, 3)).reshape(species, x_part, RANK * RANK)
    basis_y = basis_perm.reshape(y_local, count_gz, count_gy, RANK)
    basis_y = jnp.transpose(basis_y, (2, 1, 0, 3)).reshape(GRID, RANK)
    return (core_tensor, basis_z, basis_y)


def solution(mesh):
    in_specs = (P(None, "gz", "gy", None),)
    out_specs = (P(None, ("gz", "gy"), None), P(), P())
    return jax.shard_map(body, mesh=mesh, in_specs=in_specs, out_specs=out_specs, check_vma=False)
```

```python
import math

import jax
import jax.numpy as jnp
from jax import lax
from jax.experimental import pallas as pl
from jax.experimental.pallas import tpu as pltpu
from jax.sharding import PartitionSpec as P
import functools

GRID = 512
RANK = 64
ITERS = 4


def start_table(order, width):
    row_index = jnp.arange(order).astype(jnp.float32)
    col_index = jnp.arange(width).astype(jnp.float32)
    return jnp.cos(math.pi * (row_index[:, None] + 0.5) * col_index[None, :] / order)


def solve_factor(product, inner_gram):
    factor = jnp.linalg.cholesky(inner_gram)
    return lax.linalg.triangular_solve(
        factor, product, left_side=False, lower=True, transpose_a=True
    )


def inner_products(left, right):
    return lax.dot_general(left, right, (((0,), (0,)), ((), ())), precision=lax.Precision.HIGHEST)


def mode_products(left, right, mode):
    others = tuple((d for d in range(4) if d != mode))
    return lax.dot_general(
        left, right, ((others, others), ((), ())), precision=lax.Precision.HIGH
    )


def sum_over_mesh(gram):
    axes = ("gz", "gy")
    count = lax.axis_size("gz") * lax.axis_size("gy")
    rows = gram.shape[0]
    parts = lax.all_to_all(
        gram.reshape(count, rows // count, rows), axes, 0, 0, tiled=True
    )
    mine = parts.sum(0)
    tiled = jnp.broadcast_to(mine[None], (count,) + mine.shape)
    return lax.all_to_all(tiled, axes, 0, 0, tiled=True).reshape(rows, rows)


def _eliminate(c):
    n = c.shape[0]
    row = lax.broadcasted_iota(jnp.int32, (n, n), 0)
    lane = lax.broadcasted_iota(jnp.int32, (n, n), 1)
    row_col = row[:, :1]
    right = jnp.where(row == lane, 1.0, 0.0)
    diag = jnp.sum(jnp.where(row == lane, c, 0.0), axis=1, keepdims=True)

    def step(j, carry):
        left, right, diag = carry
        at_row = row == j
        row_l = jnp.sum(jnp.where(at_row, left, 0.0), axis=0, keepdims=True)
        row_r = jnp.sum(jnp.where(at_row, right, 0.0), axis=0, keepdims=True)
        col = jnp.sum(jnp.where(lane == j, left, 0.0), axis=1, keepdims=True)
        pivot = jnp.sum(jnp.where(row_col == j, diag, 0.0), axis=0, keepdims=True)
        factor = jnp.where(row_col > j, col / pivot, 0.0)
        return (left - factor * row_l, right - factor * row_r, diag - factor * col)

    _, right, diag = lax.fori_loop(0, n, step, (c, right, diag), unroll=64)
    return right / jnp.sqrt(diag)


def _basis_kernel(iters, g_ref, q_ref, out_ref):
    gram = g_ref[...]
    basis_t = q_ref[...]
    for _ in range(iters):
        product_t = jnp.dot(basis_t, gram, precision=lax.Precision.HIGHEST, preferred_element_type=jnp.float32)
        inner = lax.dot_general(product_t, product_t, (((1,), (1,)), ((), ())),
                                precision=lax.Precision.HIGHEST, preferred_element_type=jnp.float32)
        basis_t = jnp.dot(_eliminate(inner), product_t, precision=lax.Precision.HIGHEST,
                          preferred_element_type=jnp.float32)
    out_ref[...] = basis_t


def basis_pallas(gram, start, iters=4):
    size, n = start.shape
    out = pl.pallas_call(
        functools.partial(_basis_kernel, iters),
        out_shape=jax.ShapeDtypeStruct((n, size), jnp.float32),
        in_specs=[pl.BlockSpec(memory_space=pltpu.VMEM)] * 2,
        out_specs=pl.BlockSpec(memory_space=pltpu.VMEM),
    )(gram, start.T)
    return out.T

def _reduce_kernel(count, x_part, rank, fib_ref, bz_ref, out_ref, t_ref):
    y = pl.program_id(0)
    species = fib_ref.shape[1]
    per = 128 // rank
    for s in range(species):
        t_ref[s // per, :, (s % per) * rank : (s % per + 1) * rank] = jnp.dot(
            bz_ref[...], fib_ref[0, s],
            precision=lax.Precision.HIGH, preferred_element_type=jnp.float32).T
    width = species * rank
    for xl in range(x_part):
        for h in range(species // per):
            rows = t_ref[h, pl.ds(xl, count, stride=x_part), :]
            col = pl.multiple_of((y * x_part + xl) * width + h * 128, 128)
            out_ref[:, 0, pl.ds(col, 128)] = rows


def reduce_send(fib_ys, basis_z, count):
    ys, species, zs, xs = fib_ys.shape
    rank = basis_z.shape[1]
    x_part = xs // count
    return pl.pallas_call(
        functools.partial(_reduce_kernel, count, x_part, rank),
        grid=(ys,),
        in_specs=[pl.BlockSpec((1, species, zs, xs), lambda y: (y, 0, 0, 0)),
                  pl.BlockSpec((rank, zs), lambda y: (0, 0))],
        out_specs=pl.BlockSpec((count, 1, ys * x_part * species * rank), lambda y: (0, 0, 0)),
        out_shape=jax.ShapeDtypeStruct((count, 1, ys * x_part * species * rank), jnp.float32),
        scratch_shapes=[pltpu.VMEM((species * rank // 128, xs, 128), jnp.float32)],
        compiler_params=pltpu.CompilerParams(vmem_limit_bytes=48 * 1024 * 1024),
    )(fib_ys, basis_z.T)


def _gram_y_kernel(y_local, m_ref, g_ref):
    count = m_ref.shape[0]
    width = m_ref.shape[2] // y_local
    parts = [m_ref[:, 0, a * width : (a + 1) * width] for a in range(y_local)]
    for a in range(y_local):
        for b in range(y_local):
            g_ref[a * count : (a + 1) * count, b * count : (b + 1) * count] = lax.dot_general(
                parts[a], parts[b], (((1,), (1,)), ((), ())),
                precision=lax.Precision.HIGH, preferred_element_type=jnp.float32)


def gram_y_pallas(mixed, y_local):
    size = mixed.shape[0] * y_local
    return pl.pallas_call(
        functools.partial(_gram_y_kernel, y_local),
        out_shape=jax.ShapeDtypeStruct((size, size), jnp.float32),
        in_specs=[pl.BlockSpec(memory_space=pltpu.VMEM)],
        out_specs=pl.BlockSpec(memory_space=pltpu.VMEM),
    )(mixed)


def _core_kernel(y_local, m_ref, b_ref, out_ref):
    count = m_ref.shape[0]
    width = m_ref.shape[2] // y_local
    total = None
    for a in range(y_local):
        term = jnp.dot(b_ref[:, a * count : (a + 1) * count], m_ref[:, 0, a * width : (a + 1) * width],
                       precision=lax.Precision.HIGH, preferred_element_type=jnp.float32)
        total = term if total is None else total + term
    out_ref[...] = total


def core_pallas(mixed, basis_perm, y_local):
    rank = basis_perm.shape[1]
    width = mixed.shape[2] // y_local
    return pl.pallas_call(
        functools.partial(_core_kernel, y_local),
        out_shape=jax.ShapeDtypeStruct((rank, width), jnp.float32),
        in_specs=[pl.BlockSpec(memory_space=pltpu.VMEM)] * 2,
        out_specs=pl.BlockSpec(memory_space=pltpu.VMEM),
    )(mixed, basis_perm.T)


def leaf_basis(gram_part, basis_now):
    gram_total = sum_over_mesh(gram_part)
    return basis_pallas(gram_total, basis_now, ITERS)


def body(species_field):
    count_gz = lax.axis_size("gz")
    count_gy = lax.axis_size("gy")
    count = count_gz * count_gy
    fibres = lax.all_to_all(species_field, "gz", split_axis=2, concat_axis=1, tiled=True)
    species, _, y_local, x_size = fibres.shape
    gram_z = None
    for one in range(species):
        term = mode_products(fibres[one : one + 1], fibres[one : one + 1], 1)
        gram_z = term if gram_z is None else gram_z + term
    basis_z = leaf_basis(gram_z, start_table(GRID, RANK))
    x_part = x_size // count
    send = reduce_send(jnp.transpose(fibres, (2, 0, 1, 3)), basis_z, count)
    mixed = lax.all_to_all(send, ("gz", "gy"), 0, 0, tiled=True)
    gram_y = gram_y_pallas(mixed, y_local)
    start_y = start_table(GRID, RANK).reshape(count_gy, count_gz, y_local, RANK)
    start_y = jnp.transpose(start_y, (2, 1, 0, 3)).reshape(GRID, RANK)
    basis_perm = leaf_basis(gram_y, start_y)
    core_t = core_pallas(mixed, basis_perm, y_local)
    core_tensor = core_t.reshape(RANK, x_part, species, RANK)
    core_tensor = jnp.transpose(core_tensor, (2, 1, 3, 0)).reshape(species, x_part, RANK * RANK)
    basis_y = basis_perm.reshape(y_local, count_gz, count_gy, RANK)
    basis_y = jnp.transpose(basis_y, (2, 1, 0, 3)).reshape(GRID, RANK)
    return (core_tensor, basis_z, basis_y)


def solution(mesh):
    in_specs = (P(None, "gz", "gy", None),)
    out_specs = (P(None, ("gz", "gy"), None), P(), P())
    return jax.shard_map(body, mesh=mesh, in_specs=in_specs, out_specs=out_specs, check_vma=False)
```

```python
import math

import jax
import jax.numpy as jnp
from jax import lax
from jax.experimental import pallas as pl
from jax.experimental.pallas import tpu as pltpu
from jax.sharding import PartitionSpec as P
import functools

GRID = 512
RANK = 64
ITERS = 4


def start_table(order, width):
    row_index = jnp.arange(order).astype(jnp.float32)
    col_index = jnp.arange(width).astype(jnp.float32)
    return jnp.cos(math.pi * (row_index[:, None] + 0.5) * col_index[None, :] / order)


def solve_factor(product, inner_gram):
    factor = jnp.linalg.cholesky(inner_gram)
    return lax.linalg.triangular_solve(
        factor, product, left_side=False, lower=True, transpose_a=True
    )


def inner_products(left, right):
    return lax.dot_general(left, right, (((0,), (0,)), ((), ())), precision=lax.Precision.HIGHEST)


def mode_products(left, right, mode):
    others = tuple((d for d in range(4) if d != mode))
    return lax.dot_general(
        left, right, ((others, others), ((), ())), precision=lax.Precision.HIGH
    )


def sum_over_mesh(gram):
    axes = ("gz", "gy")
    count = lax.axis_size("gz") * lax.axis_size("gy")
    rows = gram.shape[0]
    parts = lax.all_to_all(
        gram.reshape(count, rows // count, rows), axes, 0, 0, tiled=True
    )
    mine = parts.sum(0)
    tiled = jnp.broadcast_to(mine[None], (count,) + mine.shape)
    return lax.all_to_all(tiled, axes, 0, 0, tiled=True).reshape(rows, rows)


def _eliminate(c):
    n = c.shape[0]
    row = lax.broadcasted_iota(jnp.int32, (n, n), 0)
    lane = lax.broadcasted_iota(jnp.int32, (n, n), 1)
    row_col = row[:, :1]
    right = jnp.where(row == lane, 1.0, 0.0)
    diag = jnp.sum(jnp.where(row == lane, c, 0.0), axis=1, keepdims=True)

    def step(j, carry):
        left, right, diag = carry
        at_row = row == j
        row_l = jnp.sum(jnp.where(at_row, left, 0.0), axis=0, keepdims=True)
        row_r = jnp.sum(jnp.where(at_row, right, 0.0), axis=0, keepdims=True)
        col = jnp.sum(jnp.where(lane == j, left, 0.0), axis=1, keepdims=True)
        pivot = jnp.sum(jnp.where(row_col == j, diag, 0.0), axis=0, keepdims=True)
        factor = jnp.where(row_col > j, col / pivot, 0.0)
        return (left - factor * row_l, right - factor * row_r, diag - factor * col)

    _, right, diag = lax.fori_loop(0, n, step, (c, right, diag), unroll=64)
    return right / jnp.sqrt(diag)


def _basis_kernel(iters, g_ref, q_ref, out_ref):
    gram = g_ref[...]
    basis_t = q_ref[...]
    for _ in range(iters):
        product_t = jnp.dot(basis_t, gram, precision=lax.Precision.HIGHEST, preferred_element_type=jnp.float32)
        inner = lax.dot_general(product_t, product_t, (((1,), (1,)), ((), ())),
                                precision=lax.Precision.HIGHEST, preferred_element_type=jnp.float32)
        basis_t = jnp.dot(_eliminate(inner), product_t, precision=lax.Precision.HIGHEST,
                          preferred_element_type=jnp.float32)
    out_ref[...] = basis_t


def basis_pallas(gram, start, iters=4):
    size, n = start.shape
    out = pl.pallas_call(
        functools.partial(_basis_kernel, iters),
        out_shape=jax.ShapeDtypeStruct((n, size), jnp.float32),
        in_specs=[pl.BlockSpec(memory_space=pltpu.VMEM)] * 2,
        out_specs=pl.BlockSpec(memory_space=pltpu.VMEM),
    )(gram, start.T)
    return out.T

def _reduce_kernel(count, x_part, rank, fib_ref, bz_ref, out_ref, t_ref):
    y = pl.program_id(0)
    species = fib_ref.shape[2]
    per = 128 // rank
    for s in range(species):
        block = fib_ref[:, 0, s]
        block = block.reshape(block.shape[0] * block.shape[1], block.shape[2])
        t_ref[s // per, :, (s % per) * rank : (s % per + 1) * rank] = jnp.dot(
            bz_ref[...], block,
            precision=lax.Precision.HIGH, preferred_element_type=jnp.float32).T
    width = species * rank
    for xl in range(x_part):
        for h in range(species // per):
            rows = t_ref[h, pl.ds(xl, count, stride=x_part), :]
            col = pl.multiple_of((y * x_part + xl) * width + h * 128, 128)
            out_ref[:, 0, pl.ds(col, 128)] = rows


def reduce_send(fib_ys, basis_z, count):
    blocks, ys, species, z_local, xs = fib_ys.shape
    zs = blocks * z_local
    rank = basis_z.shape[1]
    x_part = xs // count
    return pl.pallas_call(
        functools.partial(_reduce_kernel, count, x_part, rank),
        grid=(ys,),
        in_specs=[pl.BlockSpec((blocks, 1, species, z_local, xs), lambda y: (0, y, 0, 0, 0)),
                  pl.BlockSpec((rank, zs), lambda y: (0, 0))],
        out_specs=pl.BlockSpec((count, 1, ys * x_part * species * rank), lambda y: (0, 0, 0)),
        out_shape=jax.ShapeDtypeStruct((count, 1, ys * x_part * species * rank), jnp.float32),
        scratch_shapes=[pltpu.VMEM((species * rank // 128, xs, 128), jnp.float32)],
        compiler_params=pltpu.CompilerParams(vmem_limit_bytes=48 * 1024 * 1024),
    )(fib_ys, basis_z.T)


def _gram_z_kernel(fib_ref, g_ref):
    @pl.when((pl.program_id(0) == 0) & (pl.program_id(1) == 0))
    def _():
        g_ref[...] = jnp.zeros_like(g_ref)

    block = fib_ref[:, 0, 0]
    block = block.reshape(block.shape[0] * block.shape[1], block.shape[2])
    g_ref[...] += lax.dot_general(block, block, (((1,), (1,)), ((), ())),
                                  precision=lax.Precision.HIGH,
                                  preferred_element_type=jnp.float32)


def gram_z_pallas(fib):
    blocks, ys, species, z_local, xs = fib.shape
    size = blocks * z_local
    return pl.pallas_call(
        _gram_z_kernel,
        grid=(ys, species),
        in_specs=[pl.BlockSpec((blocks, 1, 1, z_local, xs), lambda y, s: (0, y, s, 0, 0))],
        out_specs=pl.BlockSpec((size, size), lambda y, s: (0, 0)),
        out_shape=jax.ShapeDtypeStruct((size, size), jnp.float32),
    )(fib)


def _gram_y_kernel(y_local, m_ref, g_ref):
    count = m_ref.shape[0]
    width = m_ref.shape[2] // y_local
    parts = [m_ref[:, 0, a * width : (a + 1) * width] for a in range(y_local)]
    for a in range(y_local):
        for b in range(y_local):
            g_ref[a * count : (a + 1) * count, b * count : (b + 1) * count] = lax.dot_general(
                parts[a], parts[b], (((1,), (1,)), ((), ())),
                precision=lax.Precision.HIGH, preferred_element_type=jnp.float32)


def gram_y_pallas(mixed, y_local):
    size = mixed.shape[0] * y_local
    return pl.pallas_call(
        functools.partial(_gram_y_kernel, y_local),
        out_shape=jax.ShapeDtypeStruct((size, size), jnp.float32),
        in_specs=[pl.BlockSpec(memory_space=pltpu.VMEM)],
        out_specs=pl.BlockSpec(memory_space=pltpu.VMEM),
    )(mixed)


def _core_kernel(y_local, m_ref, b_ref, out_ref):
    count = m_ref.shape[0]
    width = m_ref.shape[2] // y_local
    total = None
    for a in range(y_local):
        term = jnp.dot(b_ref[:, a * count : (a + 1) * count], m_ref[:, 0, a * width : (a + 1) * width],
                       precision=lax.Precision.HIGH, preferred_element_type=jnp.float32)
        total = term if total is None else total + term
    out_ref[...] = total


def core_pallas(mixed, basis_perm, y_local):
    rank = basis_perm.shape[1]
    width = mixed.shape[2] // y_local
    return pl.pallas_call(
        functools.partial(_core_kernel, y_local),
        out_shape=jax.ShapeDtypeStruct((rank, width), jnp.float32),
        in_specs=[pl.BlockSpec(memory_space=pltpu.VMEM)] * 2,
        out_specs=pl.BlockSpec(memory_space=pltpu.VMEM),
    )(mixed, basis_perm.T)


def leaf_basis(gram_part, basis_now):
    gram_total = sum_over_mesh(gram_part)
    return basis_pallas(gram_total, basis_now, ITERS)


def body(species_field):
    count_gz = lax.axis_size("gz")
    count_gy = lax.axis_size("gy")
    count = count_gz * count_gy
    fibres = lax.all_to_all(species_field, "gz", split_axis=2, concat_axis=1, tiled=True)
    species, _, y_local, x_size = fibres.shape
    fib5 = fibres.reshape(species, count_gz, -1, y_local, x_size)
    fib5 = jnp.transpose(fib5, (1, 3, 0, 2, 4))
    gram_z = gram_z_pallas(fib5)
    basis_z = leaf_basis(gram_z, start_table(GRID, RANK))
    x_part = x_size // count
    send = reduce_send(fib5, basis_z, count)
    mixed = lax.all_to_all(send, ("gz", "gy"), 0, 0, tiled=True)
    gram_y = gram_y_pallas(mixed, y_local)
    start_y = start_table(GRID, RANK).reshape(count_gy, count_gz, y_local, RANK)
    start_y = jnp.transpose(start_y, (2, 1, 0, 3)).reshape(GRID, RANK)
    basis_perm = leaf_basis(gram_y, start_y)
    core_t = core_pallas(mixed, basis_perm, y_local)
    core_tensor = core_t.reshape(RANK, x_part, species, RANK)
    core_tensor = jnp.transpose(core_tensor, (2, 1, 3, 0)).reshape(species, x_part, RANK * RANK)
    basis_y = basis_perm.reshape(y_local, count_gz, count_gy, RANK)
    basis_y = jnp.transpose(basis_y, (2, 1, 0, 3)).reshape(GRID, RANK)
    return (core_tensor, basis_z, basis_y)


def solution(mesh):
    in_specs = (P(None, "gz", "gy", None),)
    out_specs = (P(None, ("gz", "gy"), None), P(), P())
    return jax.shard_map(body, mesh=mesh, in_specs=in_specs, out_specs=out_specs, check_vma=False)
```

```python
import math

import jax
import jax.numpy as jnp
from jax import lax
from jax.experimental import pallas as pl
from jax.experimental.pallas import tpu as pltpu
from jax.sharding import PartitionSpec as P
import functools

GRID = 512
RANK = 64
ITERS = 4


def start_table(order, width):
    row_index = jnp.arange(order).astype(jnp.float32)
    col_index = jnp.arange(width).astype(jnp.float32)
    return jnp.cos(math.pi * (row_index[:, None] + 0.5) * col_index[None, :] / order)


def solve_factor(product, inner_gram):
    factor = jnp.linalg.cholesky(inner_gram)
    return lax.linalg.triangular_solve(
        factor, product, left_side=False, lower=True, transpose_a=True
    )


def inner_products(left, right):
    return lax.dot_general(left, right, (((0,), (0,)), ((), ())), precision=lax.Precision.HIGHEST)


def mode_products(left, right, mode):
    others = tuple((d for d in range(4) if d != mode))
    return lax.dot_general(
        left, right, ((others, others), ((), ())), precision=lax.Precision.HIGH
    )


def sum_over_mesh(gram):
    axes = ("gz", "gy")
    count = lax.axis_size("gz") * lax.axis_size("gy")
    rows = gram.shape[0]
    parts = lax.all_to_all(
        gram.reshape(count, rows // count, rows), axes, 0, 0, tiled=True
    )
    mine = parts.sum(0)
    tiled = jnp.broadcast_to(mine[None], (count,) + mine.shape)
    return lax.all_to_all(tiled, axes, 0, 0, tiled=True).reshape(rows, rows)


def _eliminate(c):
    n = c.shape[0]
    row = lax.broadcasted_iota(jnp.int32, (n, n), 0)
    lane = lax.broadcasted_iota(jnp.int32, (n, n), 1)
    row_col = row[:, :1]
    right = jnp.where(row == lane, 1.0, 0.0)
    diag = jnp.sum(jnp.where(row == lane, c, 0.0), axis=1, keepdims=True)

    def step(j, carry):
        left, right, diag = carry
        at_row = row == j
        row_l = jnp.sum(jnp.where(at_row, left, 0.0), axis=0, keepdims=True)
        row_r = jnp.sum(jnp.where(at_row, right, 0.0), axis=0, keepdims=True)
        col = jnp.sum(jnp.where(lane == j, left, 0.0), axis=1, keepdims=True)
        pivot = jnp.sum(jnp.where(row_col == j, diag, 0.0), axis=0, keepdims=True)
        factor = jnp.where(row_col > j, col / pivot, 0.0)
        return (left - factor * row_l, right - factor * row_r, diag - factor * col)

    _, right, diag = lax.fori_loop(0, n, step, (c, right, diag), unroll=64)
    return right / jnp.sqrt(diag)


def _basis_kernel(iters, g_ref, q_ref, out_ref):
    gram = g_ref[...]
    basis_t = q_ref[...]
    for _ in range(iters):
        product_t = jnp.dot(basis_t, gram, precision=lax.Precision.HIGHEST, preferred_element_type=jnp.float32)
        inner = lax.dot_general(product_t, product_t, (((1,), (1,)), ((), ())),
                                precision=lax.Precision.HIGHEST, preferred_element_type=jnp.float32)
        basis_t = jnp.dot(_eliminate(inner), product_t, precision=lax.Precision.HIGHEST,
                          preferred_element_type=jnp.float32)
    out_ref[...] = basis_t


def basis_pallas(gram, start, iters=4):
    size, n = start.shape
    out = pl.pallas_call(
        functools.partial(_basis_kernel, iters),
        out_shape=jax.ShapeDtypeStruct((n, size), jnp.float32),
        in_specs=[pl.BlockSpec(memory_space=pltpu.VMEM)] * 2,
        out_specs=pl.BlockSpec(memory_space=pltpu.VMEM),
    )(gram, start.T)
    return out.T

def _reduce_kernel(count, x_part, rank, fib_ref, bz_ref, out_ref, t_ref):
    y = pl.program_id(0)
    species = fib_ref.shape[2]
    per = 128 // rank
    for s in range(species):
        block = fib_ref[:, 0, s]
        block = block.reshape(block.shape[0] * block.shape[1], block.shape[2])
        t_ref[s // per, :, (s % per) * rank : (s % per + 1) * rank] = jnp.dot(
            bz_ref[...], block,
            precision=lax.Precision.HIGH, preferred_element_type=jnp.float32).T
    width = species * rank
    for xl in range(x_part):
        for h in range(species // per):
            rows = t_ref[h, pl.ds(xl, count, stride=x_part), :]
            col = pl.multiple_of((y * x_part + xl) * width + h * 128, 128)
            out_ref[:, 0, pl.ds(col, 128)] = rows


def reduce_send(fib_ys, basis_z, count):
    blocks, ys, species, z_local, xs = fib_ys.shape
    zs = blocks * z_local
    rank = basis_z.shape[1]
    x_part = xs // count
    return pl.pallas_call(
        functools.partial(_reduce_kernel, count, x_part, rank),
        grid=(ys,),
        in_specs=[pl.BlockSpec((blocks, 1, species, z_local, xs), lambda y: (0, y, 0, 0, 0)),
                  pl.BlockSpec((rank, zs), lambda y: (0, 0))],
        out_specs=pl.BlockSpec((count, 1, ys * x_part * species * rank), lambda y: (0, 0, 0)),
        out_shape=jax.ShapeDtypeStruct((count, 1, ys * x_part * species * rank), jnp.float32),
        scratch_shapes=[pltpu.VMEM((species * rank // 128, xs, 128), jnp.float32)],
        compiler_params=pltpu.CompilerParams(vmem_limit_bytes=48 * 1024 * 1024),
    )(fib_ys, basis_z.T)


def _gram_z_kernel(fib_ref, g_ref):
    first = (pl.program_id(0) == 0) & (pl.program_id(1) == 0)
    last = (pl.program_id(0) == pl.num_programs(0) - 1) & (
        pl.program_id(1) == pl.num_programs(1) - 1)

    @pl.when(first)
    def _():
        g_ref[...] = jnp.zeros_like(g_ref)

    block = fib_ref[:, 0, 0]
    block = block.reshape(block.shape[0] * block.shape[1], block.shape[2])
    half = block.shape[0] // 2
    for a, b in ((0, 0), (0, 1), (1, 1)):
        g_ref[a * half : (a + 1) * half, b * half : (b + 1) * half] += lax.dot_general(
            block[a * half : (a + 1) * half], block[b * half : (b + 1) * half],
            (((1,), (1,)), ((), ())), precision=lax.Precision.HIGH,
            preferred_element_type=jnp.float32)

    @pl.when(last)
    def _():
        g_ref[half:, :half] = g_ref[:half, half:].T


def gram_z_pallas(fib):
    blocks, ys, species, z_local, xs = fib.shape
    size = blocks * z_local
    return pl.pallas_call(
        _gram_z_kernel,
        grid=(ys, species),
        in_specs=[pl.BlockSpec((blocks, 1, 1, z_local, xs), lambda y, s: (0, y, s, 0, 0))],
        out_specs=pl.BlockSpec((size, size), lambda y, s: (0, 0)),
        out_shape=jax.ShapeDtypeStruct((size, size), jnp.float32),
    )(fib)


def _gram_y_kernel(y_local, m_ref, g_ref):
    count = m_ref.shape[0]
    width = m_ref.shape[2] // y_local
    parts = [m_ref[:, 0, a * width : (a + 1) * width] for a in range(y_local)]
    for a in range(y_local):
        for b in range(y_local):
            g_ref[a * count : (a + 1) * count, b * count : (b + 1) * count] = lax.dot_general(
                parts[a], parts[b], (((1,), (1,)), ((), ())),
                precision=lax.Precision.HIGH, preferred_element_type=jnp.float32)


def gram_y_pallas(mixed, y_local):
    size = mixed.shape[0] * y_local
    return pl.pallas_call(
        functools.partial(_gram_y_kernel, y_local),
        out_shape=jax.ShapeDtypeStruct((size, size), jnp.float32),
        in_specs=[pl.BlockSpec(memory_space=pltpu.VMEM)],
        out_specs=pl.BlockSpec(memory_space=pltpu.VMEM),
    )(mixed)


def _core_kernel(y_local, m_ref, b_ref, out_ref):
    count = m_ref.shape[0]
    width = m_ref.shape[2] // y_local
    total = None
    for a in range(y_local):
        term = jnp.dot(b_ref[:, a * count : (a + 1) * count], m_ref[:, 0, a * width : (a + 1) * width],
                       precision=lax.Precision.HIGH, preferred_element_type=jnp.float32)
        total = term if total is None else total + term
    out_ref[...] = total


def core_pallas(mixed, basis_perm, y_local):
    rank = basis_perm.shape[1]
    width = mixed.shape[2] // y_local
    return pl.pallas_call(
        functools.partial(_core_kernel, y_local),
        out_shape=jax.ShapeDtypeStruct((rank, width), jnp.float32),
        in_specs=[pl.BlockSpec(memory_space=pltpu.VMEM)] * 2,
        out_specs=pl.BlockSpec(memory_space=pltpu.VMEM),
    )(mixed, basis_perm.T)


def leaf_basis(gram_part, basis_now):
    gram_total = sum_over_mesh(gram_part)
    return basis_pallas(gram_total, basis_now, ITERS)


def body(species_field):
    count_gz = lax.axis_size("gz")
    count_gy = lax.axis_size("gy")
    count = count_gz * count_gy
    fibres = lax.all_to_all(species_field, "gz", split_axis=2, concat_axis=1, tiled=True)
    species, _, y_local, x_size = fibres.shape
    fib5 = fibres.reshape(species, count_gz, -1, y_local, x_size)
    fib5 = jnp.transpose(fib5, (1, 3, 0, 2, 4))
    gram_z = gram_z_pallas(fib5)
    basis_z = leaf_basis(gram_z, start_table(GRID, RANK))
    x_part = x_size // count
    send = reduce_send(fib5, basis_z, count)
    mixed = lax.all_to_all(send, ("gz", "gy"), 0, 0, tiled=True)
    gram_y = gram_y_pallas(mixed, y_local)
    start_y = start_table(GRID, RANK).reshape(count_gy, count_gz, y_local, RANK)
    start_y = jnp.transpose(start_y, (2, 1, 0, 3)).reshape(GRID, RANK)
    basis_perm = leaf_basis(gram_y, start_y)
    core_t = core_pallas(mixed, basis_perm, y_local)
    core_tensor = core_t.reshape(RANK, x_part, species, RANK)
    core_tensor = jnp.transpose(core_tensor, (2, 1, 3, 0)).reshape(species, x_part, RANK * RANK)
    basis_y = basis_perm.reshape(y_local, count_gz, count_gy, RANK)
    basis_y = jnp.transpose(basis_y, (2, 1, 0, 3)).reshape(GRID, RANK)
    return (core_tensor, basis_z, basis_y)


def solution(mesh):
    in_specs = (P(None, "gz", "gy", None),)
    out_specs = (P(None, ("gz", "gy"), None), P(), P())
    return jax.shard_map(body, mesh=mesh, in_specs=in_specs, out_specs=out_specs, check_vma=False)
```

```python
import math

import jax
import jax.numpy as jnp
from jax import lax
from jax.experimental import pallas as pl
from jax.experimental.pallas import tpu as pltpu
from jax.sharding import PartitionSpec as P
import functools

GRID = 512
RANK = 64
ITERS = 4


def start_table(order, width):
    row_index = jnp.arange(order).astype(jnp.float32)
    col_index = jnp.arange(width).astype(jnp.float32)
    return jnp.cos(math.pi * (row_index[:, None] + 0.5) * col_index[None, :] / order)


def solve_factor(product, inner_gram):
    factor = jnp.linalg.cholesky(inner_gram)
    return lax.linalg.triangular_solve(
        factor, product, left_side=False, lower=True, transpose_a=True
    )


def inner_products(left, right):
    return lax.dot_general(left, right, (((0,), (0,)), ((), ())), precision=lax.Precision.HIGHEST)


def mode_products(left, right, mode):
    others = tuple((d for d in range(4) if d != mode))
    return lax.dot_general(
        left, right, ((others, others), ((), ())), precision=lax.Precision.HIGH
    )


def sum_over_mesh(gram):
    axes = ("gz", "gy")
    count = lax.axis_size("gz") * lax.axis_size("gy")
    rows = gram.shape[0]
    parts = lax.all_to_all(
        gram.reshape(count, rows // count, rows), axes, 0, 0, tiled=True
    )
    mine = parts.sum(0)
    tiled = jnp.broadcast_to(mine[None], (count,) + mine.shape)
    return lax.all_to_all(tiled, axes, 0, 0, tiled=True).reshape(rows, rows)


def _eliminate(c):
    n = c.shape[0]
    row = lax.broadcasted_iota(jnp.int32, (n, n), 0)
    lane = lax.broadcasted_iota(jnp.int32, (n, n), 1)
    row_col = row[:, :1]
    right = jnp.where(row == lane, 1.0, 0.0)
    diag = jnp.sum(jnp.where(row == lane, c, 0.0), axis=1, keepdims=True)

    def step(j, carry):
        left, right, diag = carry
        at_row = row == j
        row_l = jnp.sum(jnp.where(at_row, left, 0.0), axis=0, keepdims=True)
        row_r = jnp.sum(jnp.where(at_row, right, 0.0), axis=0, keepdims=True)
        col = jnp.sum(jnp.where(lane == j, left, 0.0), axis=1, keepdims=True)
        pivot = jnp.sum(jnp.where(row_col == j, diag, 0.0), axis=0, keepdims=True)
        factor = jnp.where(row_col > j, col / pivot, 0.0)
        return (left - factor * row_l, right - factor * row_r, diag - factor * col)

    _, right, diag = lax.fori_loop(0, n, step, (c, right, diag), unroll=64)
    return right / jnp.sqrt(diag)


def _basis_kernel(iters, g_ref, q_ref, out_ref):
    gram = g_ref[...]
    basis_t = q_ref[...]
    for _ in range(iters):
        product_t = jnp.dot(basis_t, gram, precision=lax.Precision.HIGH, preferred_element_type=jnp.float32)
        inner = lax.dot_general(product_t, product_t, (((1,), (1,)), ((), ())),
                                precision=lax.Precision.HIGH, preferred_element_type=jnp.float32)
        basis_t = jnp.dot(_eliminate(inner), product_t, precision=lax.Precision.HIGH,
                          preferred_element_type=jnp.float32)
    out_ref[...] = basis_t


def basis_pallas(gram, start, iters=4):
    size, n = start.shape
    out = pl.pallas_call(
        functools.partial(_basis_kernel, iters),
        out_shape=jax.ShapeDtypeStruct((n, size), jnp.float32),
        in_specs=[pl.BlockSpec(memory_space=pltpu.VMEM)] * 2,
        out_specs=pl.BlockSpec(memory_space=pltpu.VMEM),
    )(gram, start.T)
    return out.T

def _reduce_kernel(count, x_part, rank, fib_ref, bz_ref, out_ref, t_ref):
    y = pl.program_id(0)
    species = fib_ref.shape[2]
    per = 128 // rank
    for s in range(species):
        block = fib_ref[:, 0, s]
        block = block.reshape(block.shape[0] * block.shape[1], block.shape[2])
        t_ref[s // per, :, (s % per) * rank : (s % per + 1) * rank] = jnp.dot(
            bz_ref[...], block,
            precision=lax.Precision.HIGH, preferred_element_type=jnp.float32).T
    width = species * rank
    for xl in range(x_part):
        for h in range(species // per):
            rows = t_ref[h, pl.ds(xl, count, stride=x_part), :]
            col = pl.multiple_of((y * x_part + xl) * width + h * 128, 128)
            out_ref[:, 0, pl.ds(col, 128)] = rows


def reduce_send(fib_ys, basis_z, count):
    blocks, ys, species, z_local, xs = fib_ys.shape
    zs = blocks * z_local
    rank = basis_z.shape[1]
    x_part = xs // count
    return pl.pallas_call(
        functools.partial(_reduce_kernel, count, x_part, rank),
        grid=(ys,),
        in_specs=[pl.BlockSpec((blocks, 1, species, z_local, xs), lambda y: (0, y, 0, 0, 0)),
                  pl.BlockSpec((rank, zs), lambda y: (0, 0))],
        out_specs=pl.BlockSpec((count, 1, ys * x_part * species * rank), lambda y: (0, 0, 0)),
        out_shape=jax.ShapeDtypeStruct((count, 1, ys * x_part * species * rank), jnp.float32),
        scratch_shapes=[pltpu.VMEM((species * rank // 128, xs, 128), jnp.float32)],
        compiler_params=pltpu.CompilerParams(vmem_limit_bytes=48 * 1024 * 1024),
    )(fib_ys, basis_z.T)


def _gram_z_kernel(fib_ref, g_ref):
    first = (pl.program_id(0) == 0) & (pl.program_id(1) == 0)
    last = (pl.program_id(0) == pl.num_programs(0) - 1) & (
        pl.program_id(1) == pl.num_programs(1) - 1)

    @pl.when(first)
    def _():
        g_ref[...] = jnp.zeros_like(g_ref)

    block = fib_ref[:, 0, 0]
    block = block.reshape(block.shape[0] * block.shape[1], block.shape[2])
    half = block.shape[0] // 2
    for a, b in ((0, 0), (0, 1), (1, 1)):
        g_ref[a * half : (a + 1) * half, b * half : (b + 1) * half] += lax.dot_general(
            block[a * half : (a + 1) * half], block[b * half : (b + 1) * half],
            (((1,), (1,)), ((), ())), precision=lax.Precision.HIGH,
            preferred_element_type=jnp.float32)

    @pl.when(last)
    def _():
        g_ref[half:, :half] = g_ref[:half, half:].T


def gram_z_pallas(fib):
    blocks, ys, species, z_local, xs = fib.shape
    size = blocks * z_local
    return pl.pallas_call(
        _gram_z_kernel,
        grid=(ys, species),
        in_specs=[pl.BlockSpec((blocks, 1, 1, z_local, xs), lambda y, s: (0, y, s, 0, 0))],
        out_specs=pl.BlockSpec((size, size), lambda y, s: (0, 0)),
        out_shape=jax.ShapeDtypeStruct((size, size), jnp.float32),
    )(fib)


def _gram_y_kernel(y_local, m_ref, g_ref):
    count = m_ref.shape[0]
    width = m_ref.shape[2] // y_local
    parts = [m_ref[:, 0, a * width : (a + 1) * width] for a in range(y_local)]
    for a in range(y_local):
        for b in range(a, y_local):
            g_ref[a * count : (a + 1) * count, b * count : (b + 1) * count] = lax.dot_general(
                parts[a], parts[b], (((1,), (1,)), ((), ())),
                precision=lax.Precision.HIGH, preferred_element_type=jnp.float32)
    for a in range(y_local):
        for b in range(a):
            g_ref[a * count : (a + 1) * count, b * count : (b + 1) * count] = (
                g_ref[b * count : (b + 1) * count, a * count : (a + 1) * count].T)


def gram_y_pallas(mixed, y_local):
    size = mixed.shape[0] * y_local
    return pl.pallas_call(
        functools.partial(_gram_y_kernel, y_local),
        out_shape=jax.ShapeDtypeStruct((size, size), jnp.float32),
        in_specs=[pl.BlockSpec(memory_space=pltpu.VMEM)],
        out_specs=pl.BlockSpec(memory_space=pltpu.VMEM),
    )(mixed)


def _core_kernel(y_local, m_ref, b_ref, out_ref):
    count = m_ref.shape[0]
    width = m_ref.shape[2] // y_local
    total = None
    for a in range(y_local):
        term = jnp.dot(b_ref[:, a * count : (a + 1) * count], m_ref[:, 0, a * width : (a + 1) * width],
                       precision=lax.Precision.HIGH, preferred_element_type=jnp.float32)
        total = term if total is None else total + term
    out_ref[...] = total


def core_pallas(mixed, basis_perm, y_local):
    rank = basis_perm.shape[1]
    width = mixed.shape[2] // y_local
    return pl.pallas_call(
        functools.partial(_core_kernel, y_local),
        out_shape=jax.ShapeDtypeStruct((rank, width), jnp.float32),
        in_specs=[pl.BlockSpec(memory_space=pltpu.VMEM)] * 2,
        out_specs=pl.BlockSpec(memory_space=pltpu.VMEM),
    )(mixed, basis_perm.T)


def leaf_basis(gram_part, basis_now):
    gram_total = sum_over_mesh(gram_part)
    return basis_pallas(gram_total, basis_now, ITERS)


def body(species_field):
    count_gz = lax.axis_size("gz")
    count_gy = lax.axis_size("gy")
    count = count_gz * count_gy
    fibres = lax.all_to_all(species_field, "gz", split_axis=2, concat_axis=1, tiled=True)
    species, _, y_local, x_size = fibres.shape
    fib5 = fibres.reshape(species, count_gz, -1, y_local, x_size)
    fib5 = jnp.transpose(fib5, (1, 3, 0, 2, 4))
    gram_z = gram_z_pallas(fib5)
    basis_z = leaf_basis(gram_z, start_table(GRID, RANK))
    x_part = x_size // count
    send = reduce_send(fib5, basis_z, count)
    mixed = lax.all_to_all(send, ("gz", "gy"), 0, 0, tiled=True)
    gram_y = gram_y_pallas(mixed, y_local)
    start_y = start_table(GRID, RANK).reshape(count_gy, count_gz, y_local, RANK)
    start_y = jnp.transpose(start_y, (2, 1, 0, 3)).reshape(GRID, RANK)
    basis_perm = leaf_basis(gram_y, start_y)
    core_t = core_pallas(mixed, basis_perm, y_local)
    core_tensor = core_t.reshape(RANK, x_part, species, RANK)
    core_tensor = jnp.transpose(core_tensor, (2, 1, 3, 0)).reshape(species, x_part, RANK * RANK)
    basis_y = basis_perm.reshape(y_local, count_gz, count_gy, RANK)
    basis_y = jnp.transpose(basis_y, (2, 1, 0, 3)).reshape(GRID, RANK)
    return (core_tensor, basis_z, basis_y)


def solution(mesh):
    in_specs = (P(None, "gz", "gy", None),)
    out_specs = (P(None, ("gz", "gy"), None), P(), P())
    return jax.shard_map(body, mesh=mesh, in_specs=in_specs, out_specs=out_specs, check_vma=False)
```

```python
import math

import jax
import jax.numpy as jnp
from jax import lax
from jax.experimental import pallas as pl
from jax.experimental.pallas import tpu as pltpu
from jax.sharding import PartitionSpec as P
import functools

GRID = 512
RANK = 64
ITERS = 4


def start_table(order, width):
    row_index = jnp.arange(order).astype(jnp.float32)
    col_index = jnp.arange(width).astype(jnp.float32)
    return jnp.cos(math.pi * (row_index[:, None] + 0.5) * col_index[None, :] / order)


def solve_factor(product, inner_gram):
    factor = jnp.linalg.cholesky(inner_gram)
    return lax.linalg.triangular_solve(
        factor, product, left_side=False, lower=True, transpose_a=True
    )


def inner_products(left, right):
    return lax.dot_general(left, right, (((0,), (0,)), ((), ())), precision=lax.Precision.HIGHEST)


def mode_products(left, right, mode):
    others = tuple((d for d in range(4) if d != mode))
    return lax.dot_general(
        left, right, ((others, others), ((), ())), precision=lax.Precision.HIGH
    )


def sum_over_mesh(gram):
    axes = ("gz", "gy")
    count = lax.axis_size("gz") * lax.axis_size("gy")
    rows = gram.shape[0]
    parts = lax.all_to_all(
        gram.reshape(count, rows // count, rows), axes, 0, 0, tiled=True
    )
    mine = parts.sum(0)
    tiled = jnp.broadcast_to(mine[None], (count,) + mine.shape)
    return lax.all_to_all(tiled, axes, 0, 0, tiled=True).reshape(rows, rows)


def _eliminate(c):
    n = c.shape[0]
    row = lax.broadcasted_iota(jnp.int32, (n, n), 0)
    lane = lax.broadcasted_iota(jnp.int32, (n, n), 1)
    row_col = row[:, :1]
    right = jnp.where(row == lane, 1.0, 0.0)
    diag = jnp.sum(jnp.where(row == lane, c, 0.0), axis=1, keepdims=True)

    def step(j, carry):
        left, right, diag = carry
        at_row = row == j
        row_l = jnp.sum(jnp.where(at_row, left, 0.0), axis=0, keepdims=True)
        row_r = jnp.sum(jnp.where(at_row, right, 0.0), axis=0, keepdims=True)
        col = jnp.sum(jnp.where(lane == j, left, 0.0), axis=1, keepdims=True)
        pivot = jnp.sum(jnp.where(row_col == j, diag, 0.0), axis=0, keepdims=True)
        factor = jnp.where(row_col > j, col / pivot, 0.0)
        return (left - factor * row_l, right - factor * row_r, diag - factor * col)

    _, right, diag = lax.fori_loop(0, n, step, (c, right, diag), unroll=32)
    return right / jnp.sqrt(diag)


def _basis_kernel(iters, g_ref, q_ref, out_ref):
    gram = g_ref[...]
    basis_t = q_ref[...]
    for _ in range(iters):
        product_t = jnp.dot(basis_t, gram, precision=lax.Precision.HIGH, preferred_element_type=jnp.float32)
        inner = lax.dot_general(product_t, product_t, (((1,), (1,)), ((), ())),
                                precision=lax.Precision.HIGH, preferred_element_type=jnp.float32)
        basis_t = jnp.dot(_eliminate(inner), product_t, precision=lax.Precision.HIGH,
                          preferred_element_type=jnp.float32)
    out_ref[...] = basis_t


def basis_pallas(gram, start, iters=4):
    size, n = start.shape
    out = pl.pallas_call(
        functools.partial(_basis_kernel, iters),
        out_shape=jax.ShapeDtypeStruct((n, size), jnp.float32),
        in_specs=[pl.BlockSpec(memory_space=pltpu.VMEM)] * 2,
        out_specs=pl.BlockSpec(memory_space=pltpu.VMEM),
    )(gram, start.T)
    return out.T

def _reduce_kernel(count, x_part, rank, fib_ref, bz_ref, out_ref, t_ref):
    y = pl.program_id(0)
    species = fib_ref.shape[2]
    per = 128 // rank
    for s in range(species):
        block = fib_ref[:, 0, s]
        block = block.reshape(block.shape[0] * block.shape[1], block.shape[2])
        t_ref[s // per, :, (s % per) * rank : (s % per + 1) * rank] = jnp.dot(
            bz_ref[...], block,
            precision=lax.Precision.HIGH, preferred_element_type=jnp.float32).T
    width = species * rank
    for xl in range(x_part):
        for h in range(species // per):
            rows = t_ref[h, pl.ds(xl, count, stride=x_part), :]
            col = pl.multiple_of((y * x_part + xl) * width + h * 128, 128)
            out_ref[:, 0, pl.ds(col, 128)] = rows


def reduce_send(fib_ys, basis_z, count):
    blocks, ys, species, z_local, xs = fib_ys.shape
    zs = blocks * z_local
    rank = basis_z.shape[1]
    x_part = xs // count
    return pl.pallas_call(
        functools.partial(_reduce_kernel, count, x_part, rank),
        grid=(ys,),
        in_specs=[pl.BlockSpec((blocks, 1, species, z_local, xs), lambda y: (0, y, 0, 0, 0)),
                  pl.BlockSpec((rank, zs), lambda y: (0, 0))],
        out_specs=pl.BlockSpec((count, 1, ys * x_part * species * rank), lambda y: (0, 0, 0)),
        out_shape=jax.ShapeDtypeStruct((count, 1, ys * x_part * species * rank), jnp.float32),
        scratch_shapes=[pltpu.VMEM((species * rank // 128, xs, 128), jnp.float32)],
        compiler_params=pltpu.CompilerParams(vmem_limit_bytes=48 * 1024 * 1024),
    )(fib_ys, basis_z.T)


def _gram_z_kernel(fib_ref, g_ref):
    first = (pl.program_id(0) == 0) & (pl.program_id(1) == 0)
    last = (pl.program_id(0) == pl.num_programs(0) - 1) & (
        pl.program_id(1) == pl.num_programs(1) - 1)

    @pl.when(first)
    def _():
        g_ref[...] = jnp.zeros_like(g_ref)

    block = fib_ref[:, 0, 0]
    block = block.reshape(block.shape[0] * block.shape[1], block.shape[2])
    half = block.shape[0] // 2
    for a, b in ((0, 0), (0, 1), (1, 1)):
        g_ref[a * half : (a + 1) * half, b * half : (b + 1) * half] += lax.dot_general(
            block[a * half : (a + 1) * half], block[b * half : (b + 1) * half],
            (((1,), (1,)), ((), ())), precision=lax.Precision.HIGH,
            preferred_element_type=jnp.float32)

    @pl.when(last)
    def _():
        g_ref[half:, :half] = g_ref[:half, half:].T


def gram_z_pallas(fib):
    blocks, ys, species, z_local, xs = fib.shape
    size = blocks * z_local
    return pl.pallas_call(
        _gram_z_kernel,
        grid=(ys, species),
        in_specs=[pl.BlockSpec((blocks, 1, 1, z_local, xs), lambda y, s: (0, y, s, 0, 0))],
        out_specs=pl.BlockSpec((size, size), lambda y, s: (0, 0)),
        out_shape=jax.ShapeDtypeStruct((size, size), jnp.float32),
    )(fib)


def _gram_y_kernel(y_local, m_ref, g_ref):
    count = m_ref.shape[0]
    width = m_ref.shape[2] // y_local
    parts = [m_ref[:, 0, a * width : (a + 1) * width] for a in range(y_local)]
    for a in range(y_local):
        for b in range(a, y_local):
            g_ref[a * count : (a + 1) * count, b * count : (b + 1) * count] = lax.dot_general(
                parts[a], parts[b], (((1,), (1,)), ((), ())),
                precision=lax.Precision.HIGH, preferred_element_type=jnp.float32)
    for a in range(y_local):
        for b in range(a):
            g_ref[a * count : (a + 1) * count, b * count : (b + 1) * count] = (
                g_ref[b * count : (b + 1) * count, a * count : (a + 1) * count].T)


def gram_y_pallas(mixed, y_local):
    size = mixed.shape[0] * y_local
    return pl.pallas_call(
        functools.partial(_gram_y_kernel, y_local),
        out_shape=jax.ShapeDtypeStruct((size, size), jnp.float32),
        in_specs=[pl.BlockSpec(memory_space=pltpu.VMEM)],
        out_specs=pl.BlockSpec(memory_space=pltpu.VMEM),
    )(mixed)


def _core_kernel(y_local, m_ref, b_ref, out_ref):
    count = m_ref.shape[0]
    width = m_ref.shape[2] // y_local
    total = None
    for a in range(y_local):
        term = jnp.dot(b_ref[:, a * count : (a + 1) * count], m_ref[:, 0, a * width : (a + 1) * width],
                       precision=lax.Precision.HIGH, preferred_element_type=jnp.float32)
        total = term if total is None else total + term
    out_ref[...] = total


def core_pallas(mixed, basis_perm, y_local):
    rank = basis_perm.shape[1]
    width = mixed.shape[2] // y_local
    return pl.pallas_call(
        functools.partial(_core_kernel, y_local),
        out_shape=jax.ShapeDtypeStruct((rank, width), jnp.float32),
        in_specs=[pl.BlockSpec(memory_space=pltpu.VMEM)] * 2,
        out_specs=pl.BlockSpec(memory_space=pltpu.VMEM),
    )(mixed, basis_perm.T)


def leaf_basis(gram_part, basis_now):
    gram_total = sum_over_mesh(gram_part)
    return basis_pallas(gram_total, basis_now, ITERS)


def body(species_field):
    count_gz = lax.axis_size("gz")
    count_gy = lax.axis_size("gy")
    count = count_gz * count_gy
    fibres = lax.all_to_all(species_field, "gz", split_axis=2, concat_axis=1, tiled=True)
    species, _, y_local, x_size = fibres.shape
    fib5 = fibres.reshape(species, count_gz, -1, y_local, x_size)
    fib5 = jnp.transpose(fib5, (1, 3, 0, 2, 4))
    gram_z = gram_z_pallas(fib5)
    basis_z = leaf_basis(gram_z, start_table(GRID, RANK))
    x_part = x_size // count
    send = reduce_send(fib5, basis_z, count)
    mixed = lax.all_to_all(send, ("gz", "gy"), 0, 0, tiled=True)
    gram_y = gram_y_pallas(mixed, y_local)
    start_y = start_table(GRID, RANK).reshape(count_gy, count_gz, y_local, RANK)
    start_y = jnp.transpose(start_y, (2, 1, 0, 3)).reshape(GRID, RANK)
    basis_perm = leaf_basis(gram_y, start_y)
    core_t = core_pallas(mixed, basis_perm, y_local)
    core_tensor = core_t.reshape(RANK, x_part, species, RANK)
    core_tensor = jnp.transpose(core_tensor, (2, 1, 3, 0)).reshape(species, x_part, RANK * RANK)
    basis_y = basis_perm.reshape(y_local, count_gz, count_gy, RANK)
    basis_y = jnp.transpose(basis_y, (2, 1, 0, 3)).reshape(GRID, RANK)
    return (core_tensor, basis_z, basis_y)


def solution(mesh):
    in_specs = (P(None, "gz", "gy", None),)
    out_specs = (P(None, ("gz", "gy"), None), P(), P())
    return jax.shard_map(body, mesh=mesh, in_specs=in_specs, out_specs=out_specs, check_vma=False)
```

```python
import math

import jax
import jax.numpy as jnp
from jax import lax
from jax.experimental import pallas as pl
from jax.experimental.pallas import tpu as pltpu
from jax.sharding import PartitionSpec as P
import functools

GRID = 512
RANK = 64
ITERS = 4


def start_table(order, width):
    row_index = jnp.arange(order).astype(jnp.float32)
    col_index = jnp.arange(width).astype(jnp.float32)
    return jnp.cos(math.pi * (row_index[:, None] + 0.5) * col_index[None, :] / order)


def solve_factor(product, inner_gram):
    factor = jnp.linalg.cholesky(inner_gram)
    return lax.linalg.triangular_solve(
        factor, product, left_side=False, lower=True, transpose_a=True
    )


def inner_products(left, right):
    return lax.dot_general(left, right, (((0,), (0,)), ((), ())), precision=lax.Precision.HIGHEST)


def mode_products(left, right, mode):
    others = tuple((d for d in range(4) if d != mode))
    return lax.dot_general(
        left, right, ((others, others), ((), ())), precision=lax.Precision.HIGH
    )


def sum_over_mesh(gram):
    axes = ("gz", "gy")
    count = lax.axis_size("gz") * lax.axis_size("gy")
    rows = gram.shape[0]
    parts = lax.all_to_all(
        gram.reshape(count, rows // count, rows), axes, 0, 0, tiled=True
    )
    mine = parts.sum(0)
    tiled = jnp.broadcast_to(mine[None], (count,) + mine.shape)
    return lax.all_to_all(tiled, axes, 0, 0, tiled=True).reshape(rows, rows)


def _eliminate(c):
    n = c.shape[0]
    row = lax.broadcasted_iota(jnp.int32, (n, n), 0)
    lane = lax.broadcasted_iota(jnp.int32, (n, n), 1)
    row_col = row[:, :1]
    right = jnp.where(row == lane, 1.0, 0.0)
    diag = jnp.sum(jnp.where(row == lane, c, 0.0), axis=1, keepdims=True)

    def step(j, carry):
        left, right, diag = carry
        at_row = row == j
        row_l = jnp.sum(jnp.where(at_row, left, 0.0), axis=0, keepdims=True)
        row_r = jnp.sum(jnp.where(at_row, right, 0.0), axis=0, keepdims=True)
        col = jnp.sum(jnp.where(lane == j, left, 0.0), axis=1, keepdims=True)
        pivot = jnp.sum(jnp.where(row_col == j, diag, 0.0), axis=0, keepdims=True)
        factor = jnp.where(row_col > j, col / pivot, 0.0)
        return (left - factor * row_l, right - factor * row_r, diag - factor * col)

    _, right, diag = lax.fori_loop(0, n, step, (c, right, diag), unroll=64)
    return right / jnp.sqrt(diag)


def _basis_kernel(iters, g_ref, q_ref, out_ref):
    gram = g_ref[...]
    basis_t = q_ref[...]
    for _ in range(iters):
        product_t = jnp.dot(basis_t, gram, precision=lax.Precision.HIGH, preferred_element_type=jnp.float32)
        inner = lax.dot_general(product_t, product_t, (((1,), (1,)), ((), ())),
                                precision=lax.Precision.HIGH, preferred_element_type=jnp.float32)
        basis_t = jnp.dot(_eliminate(inner), product_t, precision=lax.Precision.HIGH,
                          preferred_element_type=jnp.float32)
    out_ref[...] = basis_t


def basis_pallas(gram, start, iters=4):
    size, n = start.shape
    out = pl.pallas_call(
        functools.partial(_basis_kernel, iters),
        out_shape=jax.ShapeDtypeStruct((n, size), jnp.float32),
        in_specs=[pl.BlockSpec(memory_space=pltpu.VMEM)] * 2,
        out_specs=pl.BlockSpec(memory_space=pltpu.VMEM),
    )(gram, start.T)
    return out.T

def _reduce_kernel(count, x_part, rank, fib_ref, bz_ref, out_ref, t_ref):
    y = pl.program_id(0)
    species = fib_ref.shape[2]
    per = 128 // rank
    for s in range(species):
        block = fib_ref[:, 0, s]
        block = block.reshape(block.shape[0] * block.shape[1], block.shape[2])
        t_ref[s // per, :, (s % per) * rank : (s % per + 1) * rank] = jnp.dot(
            bz_ref[...], block,
            precision=lax.Precision.HIGH, preferred_element_type=jnp.float32).T
    width = species * rank
    for xl in range(x_part):
        for h in range(species // per):
            rows = t_ref[h, pl.ds(xl, count, stride=x_part), :]
            col = pl.multiple_of((y * x_part + xl) * width + h * 128, 128)
            out_ref[:, 0, pl.ds(col, 128)] = rows


def reduce_send(fib_ys, basis_z, count):
    blocks, ys, species, z_local, xs = fib_ys.shape
    zs = blocks * z_local
    rank = basis_z.shape[1]
    x_part = xs // count
    return pl.pallas_call(
        functools.partial(_reduce_kernel, count, x_part, rank),
        grid=(ys,),
        in_specs=[pl.BlockSpec((blocks, 1, species, z_local, xs), lambda y: (0, y, 0, 0, 0)),
                  pl.BlockSpec((rank, zs), lambda y: (0, 0))],
        out_specs=pl.BlockSpec((count, 1, ys * x_part * species * rank), lambda y: (0, 0, 0)),
        out_shape=jax.ShapeDtypeStruct((count, 1, ys * x_part * species * rank), jnp.float32),
        scratch_shapes=[pltpu.VMEM((species * rank // 128, xs, 128), jnp.float32)],
        compiler_params=pltpu.CompilerParams(vmem_limit_bytes=48 * 1024 * 1024),
    )(fib_ys, basis_z.T)


def _gram_z_kernel(fib_ref, g_ref):
    first = (pl.program_id(0) == 0) & (pl.program_id(1) == 0)
    last = (pl.program_id(0) == pl.num_programs(0) - 1) & (
        pl.program_id(1) == pl.num_programs(1) - 1)

    @pl.when(first)
    def _():
        g_ref[...] = jnp.zeros_like(g_ref)

    block = fib_ref[:, 0, 0]
    block = block.reshape(block.shape[0] * block.shape[1], block.shape[2])
    size = block.shape[0] // 4
    for a in range(4):
        for b in range(a, 4):
            g_ref[a * size : (a + 1) * size, b * size : (b + 1) * size] += lax.dot_general(
                block[a * size : (a + 1) * size], block[b * size : (b + 1) * size],
                (((1,), (1,)), ((), ())), precision=lax.Precision.HIGH,
                preferred_element_type=jnp.float32)

    @pl.when(last)
    def _():
        for a in range(4):
            for b in range(a):
                g_ref[a * size : (a + 1) * size, b * size : (b + 1) * size] = (
                    g_ref[b * size : (b + 1) * size, a * size : (a + 1) * size].T)


def gram_z_pallas(fib):
    blocks, ys, species, z_local, xs = fib.shape
    size = blocks * z_local
    return pl.pallas_call(
        _gram_z_kernel,
        grid=(ys, species),
        in_specs=[pl.BlockSpec((blocks, 1, 1, z_local, xs), lambda y, s: (0, y, s, 0, 0))],
        out_specs=pl.BlockSpec((size, size), lambda y, s: (0, 0)),
        out_shape=jax.ShapeDtypeStruct((size, size), jnp.float32),
    )(fib)


def _gram_y_kernel(y_local, m_ref, g_ref):
    count = m_ref.shape[0]
    width = m_ref.shape[2] // y_local
    parts = [m_ref[:, 0, a * width : (a + 1) * width] for a in range(y_local)]
    for a in range(y_local):
        for b in range(a, y_local):
            g_ref[a * count : (a + 1) * count, b * count : (b + 1) * count] = lax.dot_general(
                parts[a], parts[b], (((1,), (1,)), ((), ())),
                precision=lax.Precision.HIGH, preferred_element_type=jnp.float32)
    for a in range(y_local):
        for b in range(a):
            g_ref[a * count : (a + 1) * count, b * count : (b + 1) * count] = (
                g_ref[b * count : (b + 1) * count, a * count : (a + 1) * count].T)


def gram_y_pallas(mixed, y_local):
    size = mixed.shape[0] * y_local
    return pl.pallas_call(
        functools.partial(_gram_y_kernel, y_local),
        out_shape=jax.ShapeDtypeStruct((size, size), jnp.float32),
        in_specs=[pl.BlockSpec(memory_space=pltpu.VMEM)],
        out_specs=pl.BlockSpec(memory_space=pltpu.VMEM),
    )(mixed)


def _core_kernel(y_local, m_ref, b_ref, out_ref):
    count = m_ref.shape[0]
    width = m_ref.shape[2] // y_local
    total = None
    for a in range(y_local):
        term = jnp.dot(b_ref[:, a * count : (a + 1) * count], m_ref[:, 0, a * width : (a + 1) * width],
                       precision=lax.Precision.HIGH, preferred_element_type=jnp.float32)
        total = term if total is None else total + term
    out_ref[...] = total


def core_pallas(mixed, basis_perm, y_local):
    rank = basis_perm.shape[1]
    width = mixed.shape[2] // y_local
    return pl.pallas_call(
        functools.partial(_core_kernel, y_local),
        out_shape=jax.ShapeDtypeStruct((rank, width), jnp.float32),
        in_specs=[pl.BlockSpec(memory_space=pltpu.VMEM)] * 2,
        out_specs=pl.BlockSpec(memory_space=pltpu.VMEM),
    )(mixed, basis_perm.T)


def leaf_basis(gram_part, basis_now):
    gram_total = sum_over_mesh(gram_part)
    return basis_pallas(gram_total, basis_now, ITERS)


def body(species_field):
    count_gz = lax.axis_size("gz")
    count_gy = lax.axis_size("gy")
    count = count_gz * count_gy
    fibres = lax.all_to_all(species_field, "gz", split_axis=2, concat_axis=1, tiled=True)
    species, _, y_local, x_size = fibres.shape
    fib5 = fibres.reshape(species, count_gz, -1, y_local, x_size)
    fib5 = jnp.transpose(fib5, (1, 3, 0, 2, 4))
    gram_z = gram_z_pallas(fib5)
    basis_z = leaf_basis(gram_z, start_table(GRID, RANK))
    x_part = x_size // count
    send = reduce_send(fib5, basis_z, count)
    mixed = lax.all_to_all(send, ("gz", "gy"), 0, 0, tiled=True)
    gram_y = gram_y_pallas(mixed, y_local)
    start_y = start_table(GRID, RANK).reshape(count_gy, count_gz, y_local, RANK)
    start_y = jnp.transpose(start_y, (2, 1, 0, 3)).reshape(GRID, RANK)
    basis_perm = leaf_basis(gram_y, start_y)
    core_t = core_pallas(mixed, basis_perm, y_local)
    core_tensor = core_t.reshape(RANK, x_part, species, RANK)
    core_tensor = jnp.transpose(core_tensor, (2, 1, 3, 0)).reshape(species, x_part, RANK * RANK)
    basis_y = basis_perm.reshape(y_local, count_gz, count_gy, RANK)
    basis_y = jnp.transpose(basis_y, (2, 1, 0, 3)).reshape(GRID, RANK)
    return (core_tensor, basis_z, basis_y)


def solution(mesh):
    in_specs = (P(None, "gz", "gy", None),)
    out_specs = (P(None, ("gz", "gy"), None), P(), P())
    return jax.shard_map(body, mesh=mesh, in_specs=in_specs, out_specs=out_specs, check_vma=False)
```

```python
import math

import jax
import jax.numpy as jnp
from jax import lax
from jax.experimental import pallas as pl
from jax.experimental.pallas import tpu as pltpu
from jax.sharding import PartitionSpec as P
import functools

GRID = 512
RANK = 64
ITERS = 4


def start_table(order, width):
    row_index = jnp.arange(order).astype(jnp.float32)
    col_index = jnp.arange(width).astype(jnp.float32)
    return jnp.cos(math.pi * (row_index[:, None] + 0.5) * col_index[None, :] / order)


def solve_factor(product, inner_gram):
    factor = jnp.linalg.cholesky(inner_gram)
    return lax.linalg.triangular_solve(
        factor, product, left_side=False, lower=True, transpose_a=True
    )


def inner_products(left, right):
    return lax.dot_general(left, right, (((0,), (0,)), ((), ())), precision=lax.Precision.HIGHEST)


def mode_products(left, right, mode):
    others = tuple((d for d in range(4) if d != mode))
    return lax.dot_general(
        left, right, ((others, others), ((), ())), precision=lax.Precision.HIGH
    )


def sum_over_mesh(gram):
    axes = ("gz", "gy")
    count = lax.axis_size("gz") * lax.axis_size("gy")
    rows = gram.shape[0]
    if gram.ndim == 2:
        gram = gram.reshape(count, rows // count, rows)
    else:
        rows = gram.shape[2]
    parts = lax.all_to_all(gram, axes, 0, 0, tiled=True)
    mine = parts.sum(0)
    tiled = jnp.broadcast_to(mine[None], (count,) + mine.shape)
    return lax.all_to_all(tiled, axes, 0, 0, tiled=True).reshape(rows, rows)


def _eliminate(c):
    n = c.shape[0]
    row = lax.broadcasted_iota(jnp.int32, (n, n), 0)
    lane = lax.broadcasted_iota(jnp.int32, (n, n), 1)
    row_col = row[:, :1]
    right = jnp.where(row == lane, 1.0, 0.0)
    diag = jnp.sum(jnp.where(row == lane, c, 0.0), axis=1, keepdims=True)

    def step(j, carry):
        left, right, diag = carry
        at_row = row == j
        row_l = jnp.sum(jnp.where(at_row, left, 0.0), axis=0, keepdims=True)
        row_r = jnp.sum(jnp.where(at_row, right, 0.0), axis=0, keepdims=True)
        col = jnp.sum(jnp.where(lane == j, left, 0.0), axis=1, keepdims=True)
        pivot = jnp.sum(jnp.where(row_col == j, diag, 0.0), axis=0, keepdims=True)
        factor = jnp.where(row_col > j, col / pivot, 0.0)
        return (left - factor * row_l, right - factor * row_r, diag - factor * col)

    _, right, diag = lax.fori_loop(0, n, step, (c, right, diag), unroll=64)
    return right / jnp.sqrt(diag)


def _basis_kernel(iters, g_ref, q_ref, out_ref):
    gram = g_ref[...]
    basis_t = q_ref[...]
    for _ in range(iters):
        product_t = jnp.dot(basis_t, gram, precision=lax.Precision.HIGH, preferred_element_type=jnp.float32)
        inner = lax.dot_general(product_t, product_t, (((1,), (1,)), ((), ())),
                                precision=lax.Precision.HIGH, preferred_element_type=jnp.float32)
        basis_t = jnp.dot(_eliminate(inner), product_t, precision=lax.Precision.HIGH,
                          preferred_element_type=jnp.float32)
    out_ref[...] = basis_t


def basis_pallas(gram, start, iters=4):
    size, n = start.shape
    out = pl.pallas_call(
        functools.partial(_basis_kernel, iters),
        out_shape=jax.ShapeDtypeStruct((n, size), jnp.float32),
        in_specs=[pl.BlockSpec(memory_space=pltpu.VMEM)] * 2,
        out_specs=pl.BlockSpec(memory_space=pltpu.VMEM),
    )(gram, start.T)
    return out.T

def _reduce_kernel(count, x_part, rank, fib_ref, bz_ref, out_ref, t_ref):
    y = pl.program_id(0)
    species = fib_ref.shape[2]
    per = 128 // rank
    for s in range(species):
        block = fib_ref[:, 0, s]
        block = block.reshape(block.shape[0] * block.shape[1], block.shape[2])
        t_ref[s // per, :, (s % per) * rank : (s % per + 1) * rank] = jnp.dot(
            bz_ref[...], block,
            precision=lax.Precision.HIGH, preferred_element_type=jnp.float32).T
    width = species * rank
    for xl in range(x_part):
        for h in range(species // per):
            rows = t_ref[h, pl.ds(xl, count, stride=x_part), :]
            col = pl.multiple_of((y * x_part + xl) * width + h * 128, 128)
            out_ref[:, 0, pl.ds(col, 128)] = rows


def reduce_send(fib_ys, basis_z, count):
    blocks, ys, species, z_local, xs = fib_ys.shape
    zs = blocks * z_local
    rank = basis_z.shape[1]
    x_part = xs // count
    return pl.pallas_call(
        functools.partial(_reduce_kernel, count, x_part, rank),
        grid=(ys,),
        in_specs=[pl.BlockSpec((blocks, 1, species, z_local, xs), lambda y: (0, y, 0, 0, 0)),
                  pl.BlockSpec((rank, zs), lambda y: (0, 0))],
        out_specs=pl.BlockSpec((count, 1, ys * x_part * species * rank), lambda y: (0, 0, 0)),
        out_shape=jax.ShapeDtypeStruct((count, 1, ys * x_part * species * rank), jnp.float32),
        scratch_shapes=[pltpu.VMEM((species * rank // 128, xs, 128), jnp.float32)],
        compiler_params=pltpu.CompilerParams(vmem_limit_bytes=48 * 1024 * 1024),
    )(fib_ys, basis_z.T)


def _gram_z_kernel(fib_ref, g_ref):
    first = (pl.program_id(0) == 0) & (pl.program_id(1) == 0)
    last = (pl.program_id(0) == pl.num_programs(0) - 1) & (
        pl.program_id(1) == pl.num_programs(1) - 1)

    @pl.when(first)
    def _():
        g_ref[...] = jnp.zeros_like(g_ref)

    block = fib_ref[:, 0, 0]
    block = block.reshape(block.shape[0] * block.shape[1], block.shape[2])
    half = block.shape[0] // 2
    for a, b in ((0, 0), (0, 1), (1, 1)):
        g_ref[a * half : (a + 1) * half, b * half : (b + 1) * half] += lax.dot_general(
            block[a * half : (a + 1) * half], block[b * half : (b + 1) * half],
            (((1,), (1,)), ((), ())), precision=lax.Precision.HIGH,
            preferred_element_type=jnp.float32)

    @pl.when(last)
    def _():
        g_ref[half:, :half] = g_ref[:half, half:].T


def gram_z_pallas(fib):
    blocks, ys, species, z_local, xs = fib.shape
    size = blocks * z_local
    return pl.pallas_call(
        _gram_z_kernel,
        grid=(ys, species),
        in_specs=[pl.BlockSpec((blocks, 1, 1, z_local, xs), lambda y, s: (0, y, s, 0, 0))],
        out_specs=pl.BlockSpec((size, size), lambda y, s: (0, 0)),
        out_shape=jax.ShapeDtypeStruct((size, size), jnp.float32),
    )(fib)


def _gram_y_kernel(y_local, m_ref, g_ref):
    count = m_ref.shape[0]
    width = m_ref.shape[2] // y_local
    rows = count // y_local
    parts = [m_ref[:, 0, a * width : (a + 1) * width] for a in range(y_local)]
    blocks = {}
    for a in range(y_local):
        for b in range(a, y_local):
            blocks[a, b] = lax.dot_general(
                parts[a], parts[b], (((1,), (1,)), ((), ())),
                precision=lax.Precision.HIGH, preferred_element_type=jnp.float32)
    for a in range(y_local):
        for b in range(a):
            blocks[a, b] = blocks[b, a].T
    for a in range(y_local):
        g_ref[a * rows : (a + 1) * rows] = jnp.concatenate(
            [blocks[a, b] for b in range(y_local)], axis=1).reshape(rows, y_local, -1)


def gram_y_pallas(mixed, y_local):
    count = mixed.shape[0]
    size = count * y_local
    return pl.pallas_call(
        functools.partial(_gram_y_kernel, y_local),
        out_shape=jax.ShapeDtypeStruct((count, y_local, size), jnp.float32),
        in_specs=[pl.BlockSpec(memory_space=pltpu.VMEM)],
        out_specs=pl.BlockSpec(memory_space=pltpu.VMEM),
    )(mixed)


def _core_kernel(y_local, m_ref, b_ref, out_ref):
    count = m_ref.shape[0]
    width = m_ref.shape[2] // y_local
    total = None
    for a in range(y_local):
        term = jnp.dot(b_ref[:, a * count : (a + 1) * count], m_ref[:, 0, a * width : (a + 1) * width],
                       precision=lax.Precision.HIGH, preferred_element_type=jnp.float32)
        total = term if total is None else total + term
    out_ref[...] = total


def core_pallas(mixed, basis_perm, y_local):
    rank = basis_perm.shape[1]
    width = mixed.shape[2] // y_local
    return pl.pallas_call(
        functools.partial(_core_kernel, y_local),
        out_shape=jax.ShapeDtypeStruct((rank, width), jnp.float32),
        in_specs=[pl.BlockSpec(memory_space=pltpu.VMEM)] * 2,
        out_specs=pl.BlockSpec(memory_space=pltpu.VMEM),
    )(mixed, basis_perm.T)


def leaf_basis(gram_part, basis_now):
    gram_total = sum_over_mesh(gram_part)
    return basis_pallas(gram_total, basis_now, ITERS)


def body(species_field):
    count_gz = lax.axis_size("gz")
    count_gy = lax.axis_size("gy")
    count = count_gz * count_gy
    fibres = lax.all_to_all(species_field, "gz", split_axis=2, concat_axis=1, tiled=True)
    species, _, y_local, x_size = fibres.shape
    fib5 = fibres.reshape(species, count_gz, -1, y_local, x_size)
    fib5 = jnp.transpose(fib5, (1, 3, 0, 2, 4))
    gram_z = gram_z_pallas(fib5)
    basis_z = leaf_basis(gram_z, start_table(GRID, RANK))
    x_part = x_size // count
    send = reduce_send(fib5, basis_z, count)
    mixed = lax.all_to_all(send, ("gz", "gy"), 0, 0, tiled=True)
    gram_y = gram_y_pallas(mixed, y_local)
    start_y = start_table(GRID, RANK).reshape(count_gy, count_gz, y_local, RANK)
    start_y = jnp.transpose(start_y, (2, 1, 0, 3)).reshape(GRID, RANK)
    basis_perm = leaf_basis(gram_y, start_y)
    core_t = core_pallas(mixed, basis_perm, y_local)
    core_tensor = core_t.reshape(RANK, x_part, species, RANK)
    core_tensor = jnp.transpose(core_tensor, (2, 1, 3, 0)).reshape(species, x_part, RANK * RANK)
    basis_y = basis_perm.reshape(y_local, count_gz, count_gy, RANK)
    basis_y = jnp.transpose(basis_y, (2, 1, 0, 3)).reshape(GRID, RANK)
    return (core_tensor, basis_z, basis_y)


def solution(mesh):
    in_specs = (P(None, "gz", "gy", None),)
    out_specs = (P(None, ("gz", "gy"), None), P(), P())
    return jax.shard_map(body, mesh=mesh, in_specs=in_specs, out_specs=out_specs, check_vma=False)
```

```python
import math

import jax
import jax.numpy as jnp
from jax import lax
from jax.experimental import pallas as pl
from jax.experimental.pallas import tpu as pltpu
from jax.sharding import PartitionSpec as P
import functools

GRID = 512
RANK = 64
ITERS = 4


def start_table(order, width):
    row_index = jnp.arange(order).astype(jnp.float32)
    col_index = jnp.arange(width).astype(jnp.float32)
    return jnp.cos(math.pi * (row_index[:, None] + 0.5) * col_index[None, :] / order)


def solve_factor(product, inner_gram):
    factor = jnp.linalg.cholesky(inner_gram)
    return lax.linalg.triangular_solve(
        factor, product, left_side=False, lower=True, transpose_a=True
    )


def inner_products(left, right):
    return lax.dot_general(left, right, (((0,), (0,)), ((), ())), precision=lax.Precision.HIGHEST)


def mode_products(left, right, mode):
    others = tuple((d for d in range(4) if d != mode))
    return lax.dot_general(
        left, right, ((others, others), ((), ())), precision=lax.Precision.HIGH
    )


def sum_over_mesh(gram):
    axes = ("gz", "gy")
    count = lax.axis_size("gz") * lax.axis_size("gy")
    rows = gram.shape[0]
    parts = lax.all_to_all(
        gram.reshape(count, rows // count, rows), axes, 0, 0, tiled=True
    )
    mine = parts.sum(0)
    tiled = jnp.broadcast_to(mine[None], (count,) + mine.shape)
    return lax.all_to_all(tiled, axes, 0, 0, tiled=True)


def _eliminate(c):
    n = c.shape[0]
    row = lax.broadcasted_iota(jnp.int32, (n, n), 0)
    lane = lax.broadcasted_iota(jnp.int32, (n, n), 1)
    row_col = row[:, :1]
    right = jnp.where(row == lane, 1.0, 0.0)
    diag = jnp.sum(jnp.where(row == lane, c, 0.0), axis=1, keepdims=True)

    def step(j, carry):
        left, right, diag = carry
        at_row = row == j
        row_l = jnp.sum(jnp.where(at_row, left, 0.0), axis=0, keepdims=True)
        row_r = jnp.sum(jnp.where(at_row, right, 0.0), axis=0, keepdims=True)
        col = jnp.sum(jnp.where(lane == j, left, 0.0), axis=1, keepdims=True)
        pivot = jnp.sum(jnp.where(row_col == j, diag, 0.0), axis=0, keepdims=True)
        factor = jnp.where(row_col > j, col / pivot, 0.0)
        return (left - factor * row_l, right - factor * row_r, diag - factor * col)

    _, right, diag = lax.fori_loop(0, n - 1, step, (c, right, diag), unroll=64)
    return right / jnp.sqrt(diag)


def _basis_kernel(iters, g_ref, q_ref, out_ref):
    gram = g_ref[...]
    gram = gram.reshape(gram.shape[0] * gram.shape[1], gram.shape[2])
    basis_t = q_ref[...]
    for _ in range(iters):
        product_t = jnp.dot(basis_t, gram, precision=lax.Precision.HIGH, preferred_element_type=jnp.float32)
        inner = lax.dot_general(product_t, product_t, (((1,), (1,)), ((), ())),
                                precision=lax.Precision.HIGH, preferred_element_type=jnp.float32)
        basis_t = jnp.dot(_eliminate(inner), product_t, precision=lax.Precision.HIGH,
                          preferred_element_type=jnp.float32)
    out_ref[...] = basis_t


def basis_pallas(gram, start, iters=4):
    size, n = start.shape
    out = pl.pallas_call(
        functools.partial(_basis_kernel, iters),
        out_shape=jax.ShapeDtypeStruct((n, size), jnp.float32),
        in_specs=[pl.BlockSpec(memory_space=pltpu.VMEM)] * 2,
        out_specs=pl.BlockSpec(memory_space=pltpu.VMEM),
    )(gram, start.T)
    return out.T

def _reduce_kernel(count, x_part, rank, fib_ref, bz_ref, out_ref, t_ref):
    y = pl.program_id(0)
    species = fib_ref.shape[2]
    per = 128 // rank
    for s in range(species):
        block = fib_ref[:, 0, s]
        block = block.reshape(block.shape[0] * block.shape[1], block.shape[2])
        t_ref[s // per, :, (s % per) * rank : (s % per + 1) * rank] = jnp.dot(
            bz_ref[...], block,
            precision=lax.Precision.HIGH, preferred_element_type=jnp.float32).T
    width = species * rank
    for xl in range(x_part):
        for h in range(species // per):
            rows = t_ref[h, pl.ds(xl, count, stride=x_part), :]
            col = pl.multiple_of((y * x_part + xl) * width + h * 128, 128)
            out_ref[:, 0, pl.ds(col, 128)] = rows


def reduce_send(fib_ys, basis_z, count):
    blocks, ys, species, z_local, xs = fib_ys.shape
    zs = blocks * z_local
    rank = basis_z.shape[1]
    x_part = xs // count
    return pl.pallas_call(
        functools.partial(_reduce_kernel, count, x_part, rank),
        grid=(ys,),
        in_specs=[pl.BlockSpec((blocks, 1, species, z_local, xs), lambda y: (0, y, 0, 0, 0)),
                  pl.BlockSpec((rank, zs), lambda y: (0, 0))],
        out_specs=pl.BlockSpec((count, 1, ys * x_part * species * rank), lambda y: (0, 0, 0)),
        out_shape=jax.ShapeDtypeStruct((count, 1, ys * x_part * species * rank), jnp.float32),
        scratch_shapes=[pltpu.VMEM((species * rank // 128, xs, 128), jnp.float32)],
        compiler_params=pltpu.CompilerParams(vmem_limit_bytes=48 * 1024 * 1024),
    )(fib_ys, basis_z.T)


def _gram_z_kernel(fib_ref, g_ref):
    first = (pl.program_id(0) == 0) & (pl.program_id(1) == 0)
    last = (pl.program_id(0) == pl.num_programs(0) - 1) & (
        pl.program_id(1) == pl.num_programs(1) - 1)

    @pl.when(first)
    def _():
        g_ref[...] = jnp.zeros_like(g_ref)

    block = fib_ref[:, 0, 0]
    block = block.reshape(block.shape[0] * block.shape[1], block.shape[2])
    half = block.shape[0] // 2
    for a, b in ((0, 0), (0, 1), (1, 1)):
        g_ref[a * half : (a + 1) * half, b * half : (b + 1) * half] += lax.dot_general(
            block[a * half : (a + 1) * half], block[b * half : (b + 1) * half],
            (((1,), (1,)), ((), ())), precision=lax.Precision.HIGH,
            preferred_element_type=jnp.float32)

    @pl.when(last)
    def _():
        g_ref[half:, :half] = g_ref[:half, half:].T


def gram_z_pallas(fib):
    blocks, ys, species, z_local, xs = fib.shape
    size = blocks * z_local
    return pl.pallas_call(
        _gram_z_kernel,
        grid=(ys, species),
        in_specs=[pl.BlockSpec((blocks, 1, 1, z_local, xs), lambda y, s: (0, y, s, 0, 0))],
        out_specs=pl.BlockSpec((size, size), lambda y, s: (0, 0)),
        out_shape=jax.ShapeDtypeStruct((size, size), jnp.float32),
    )(fib)


def _gram_y_kernel(y_local, m_ref, g_ref):
    count = m_ref.shape[0]
    width = m_ref.shape[2] // y_local
    parts = [m_ref[:, 0, a * width : (a + 1) * width] for a in range(y_local)]
    for a in range(y_local):
        for b in range(a, y_local):
            g_ref[a * count : (a + 1) * count, b * count : (b + 1) * count] = lax.dot_general(
                parts[a], parts[b], (((1,), (1,)), ((), ())),
                precision=lax.Precision.HIGH, preferred_element_type=jnp.float32)
    for a in range(y_local):
        for b in range(a):
            g_ref[a * count : (a + 1) * count, b * count : (b + 1) * count] = (
                g_ref[b * count : (b + 1) * count, a * count : (a + 1) * count].T)


def gram_y_pallas(mixed, y_local):
    size = mixed.shape[0] * y_local
    return pl.pallas_call(
        functools.partial(_gram_y_kernel, y_local),
        out_shape=jax.ShapeDtypeStruct((size, size), jnp.float32),
        in_specs=[pl.BlockSpec(memory_space=pltpu.VMEM)],
        out_specs=pl.BlockSpec(memory_space=pltpu.VMEM),
    )(mixed)


def _core_kernel(y_local, m_ref, b_ref, out_ref):
    count = m_ref.shape[0]
    width = m_ref.shape[2] // y_local
    total = None
    for a in range(y_local):
        term = jnp.dot(b_ref[:, a * count : (a + 1) * count], m_ref[:, 0, a * width : (a + 1) * width],
                       precision=lax.Precision.HIGH, preferred_element_type=jnp.float32)
        total = term if total is None else total + term
    out_ref[...] = total


def core_pallas(mixed, basis_perm, y_local):
    rank = basis_perm.shape[1]
    width = mixed.shape[2] // y_local
    return pl.pallas_call(
        functools.partial(_core_kernel, y_local),
        out_shape=jax.ShapeDtypeStruct((rank, width), jnp.float32),
        in_specs=[pl.BlockSpec(memory_space=pltpu.VMEM)] * 2,
        out_specs=pl.BlockSpec(memory_space=pltpu.VMEM),
    )(mixed, basis_perm.T)


def leaf_basis(gram_part, basis_now):
    gram_total = sum_over_mesh(gram_part)
    return basis_pallas(gram_total, basis_now, ITERS)


def body(species_field):
    count_gz = lax.axis_size("gz")
    count_gy = lax.axis_size("gy")
    count = count_gz * count_gy
    fibres = lax.all_to_all(species_field, "gz", split_axis=2, concat_axis=1, tiled=True)
    species, _, y_local, x_size = fibres.shape
    fib5 = fibres.reshape(species, count_gz, -1, y_local, x_size)
    fib5 = jnp.transpose(fib5, (1, 3, 0, 2, 4))
    gram_z = gram_z_pallas(fib5)
    basis_z = leaf_basis(gram_z, start_table(GRID, RANK))
    x_part = x_size // count
    send = reduce_send(fib5, basis_z, count)
    mixed = lax.all_to_all(send, ("gz", "gy"), 0, 0, tiled=True)
    gram_y = gram_y_pallas(mixed, y_local)
    start_y = start_table(GRID, RANK).reshape(count_gy, count_gz, y_local, RANK)
    start_y = jnp.transpose(start_y, (2, 1, 0, 3)).reshape(GRID, RANK)
    basis_perm = leaf_basis(gram_y, start_y)
    core_t = core_pallas(mixed, basis_perm, y_local)
    core_tensor = core_t.reshape(RANK, x_part, species, RANK)
    core_tensor = jnp.transpose(core_tensor, (2, 1, 3, 0)).reshape(species, x_part, RANK * RANK)
    basis_y = basis_perm.reshape(y_local, count_gz, count_gy, RANK)
    basis_y = jnp.transpose(basis_y, (2, 1, 0, 3)).reshape(GRID, RANK)
    return (core_tensor, basis_z, basis_y)


def solution(mesh):
    in_specs = (P(None, "gz", "gy", None),)
    out_specs = (P(None, ("gz", "gy"), None), P(), P())
    return jax.shard_map(body, mesh=mesh, in_specs=in_specs, out_specs=out_specs, check_vma=False)
```

```python
import math

import jax
import jax.numpy as jnp
from jax import lax
from jax.experimental import pallas as pl
from jax.experimental.pallas import tpu as pltpu
from jax.sharding import PartitionSpec as P
import functools

GRID = 512
RANK = 64
ITERS = 4


def start_table(order, width):
    row_index = jnp.arange(order).astype(jnp.float32)
    col_index = jnp.arange(width).astype(jnp.float32)
    return jnp.cos(math.pi * (row_index[:, None] + 0.5) * col_index[None, :] / order)


def solve_factor(product, inner_gram):
    factor = jnp.linalg.cholesky(inner_gram)
    return lax.linalg.triangular_solve(
        factor, product, left_side=False, lower=True, transpose_a=True
    )


def inner_products(left, right):
    return lax.dot_general(left, right, (((0,), (0,)), ((), ())), precision=lax.Precision.HIGHEST)


def mode_products(left, right, mode):
    others = tuple((d for d in range(4) if d != mode))
    return lax.dot_general(
        left, right, ((others, others), ((), ())), precision=lax.Precision.HIGH
    )


def sum_over_mesh(gram):
    axes = ("gz", "gy")
    count = lax.axis_size("gz") * lax.axis_size("gy")
    rows = gram.shape[0]
    parts = lax.all_to_all(
        gram.reshape(count, rows // count, rows), axes, 0, 0, tiled=True
    )
    mine = parts.sum(0)
    tiled = jnp.broadcast_to(mine[None], (count,) + mine.shape)
    return lax.all_to_all(tiled, axes, 0, 0, tiled=True)


def _eliminate(c):
    n = c.shape[0]
    row = lax.broadcasted_iota(jnp.int32, (n, n), 0)
    lane = lax.broadcasted_iota(jnp.int32, (n, n), 1)
    row_col = row[:, :1]
    right = jnp.where(row == lane, 1.0, 0.0)
    diag = jnp.sum(jnp.where(row == lane, c, 0.0), axis=1, keepdims=True)

    def step(j, carry):
        left, right, diag = carry
        at_row = row == j
        row_l = jnp.sum(jnp.where(at_row, left, 0.0), axis=0, keepdims=True)
        row_r = jnp.sum(jnp.where(at_row, right, 0.0), axis=0, keepdims=True)
        col = jnp.sum(jnp.where(lane == j, left, 0.0), axis=1, keepdims=True)
        pivot = jnp.sum(jnp.where(row_col == j, diag, 0.0), axis=0, keepdims=True)
        factor = jnp.where(row_col > j, col / pivot, 0.0)
        return (left - factor * row_l, right - factor * row_r, diag - factor * col)

    _, right, diag = lax.fori_loop(0, n, step, (c, right, diag), unroll=64)
    return right / jnp.sqrt(diag)


def _basis_kernel(iters, g_ref, q_ref, out_ref):
    gram = g_ref[...]
    gram = gram.reshape(gram.shape[0] * gram.shape[1], gram.shape[2])
    basis_t = q_ref[...]
    for _ in range(iters):
        product_t = jnp.dot(basis_t, gram, precision=lax.Precision.HIGH, preferred_element_type=jnp.float32)
        inner = lax.dot_general(product_t, product_t, (((1,), (1,)), ((), ())),
                                precision=lax.Precision.HIGH, preferred_element_type=jnp.float32)
        basis_t = jnp.dot(_eliminate(inner), product_t, precision=lax.Precision.HIGH,
                          preferred_element_type=jnp.float32)
    out_ref[...] = basis_t


def basis_pallas(gram, start, iters=4):
    size, n = start.shape
    out = pl.pallas_call(
        functools.partial(_basis_kernel, iters),
        out_shape=jax.ShapeDtypeStruct((n, size), jnp.float32),
        in_specs=[pl.BlockSpec(memory_space=pltpu.VMEM)] * 2,
        out_specs=pl.BlockSpec(memory_space=pltpu.VMEM),
    )(gram, start.T)
    return out.T

def _reduce_kernel(count, x_part, rank, fib_ref, bz_ref, out_ref, t_ref):
    y = pl.program_id(0)
    species = fib_ref.shape[2]
    per = 128 // rank
    for s in range(species):
        block = fib_ref[:, 0, s]
        block = block.reshape(block.shape[0] * block.shape[1], block.shape[2])
        t_ref[s // per, :, (s % per) * rank : (s % per + 1) * rank] = jnp.dot(
            bz_ref[...], block,
            precision=lax.Precision.HIGH, preferred_element_type=jnp.float32).T
    width = species * rank
    for xl in range(x_part):
        for h in range(species // per):
            rows = t_ref[h, pl.ds(xl, count, stride=x_part), :]
            col = pl.multiple_of((y * x_part + xl) * width + h * 128, 128)
            out_ref[:, 0, pl.ds(col, 128)] = rows


def reduce_send(fib_ys, basis_z, count):
    blocks, ys, species, z_local, xs = fib_ys.shape
    zs = blocks * z_local
    rank = basis_z.shape[1]
    x_part = xs // count
    return pl.pallas_call(
        functools.partial(_reduce_kernel, count, x_part, rank),
        grid=(ys,),
        in_specs=[pl.BlockSpec((blocks, 1, species, z_local, xs), lambda y: (0, y, 0, 0, 0)),
                  pl.BlockSpec((rank, zs), lambda y: (0, 0))],
        out_specs=pl.BlockSpec((count, 1, ys * x_part * species * rank), lambda y: (0, 0, 0)),
        out_shape=jax.ShapeDtypeStruct((count, 1, ys * x_part * species * rank), jnp.float32),
        scratch_shapes=[pltpu.VMEM((species * rank // 128, xs, 128), jnp.float32)],
        compiler_params=pltpu.CompilerParams(vmem_limit_bytes=48 * 1024 * 1024),
    )(fib_ys, basis_z.T)


def _gram_z_kernel(fib_ref, g_ref):
    first = (pl.program_id(0) == 0) & (pl.program_id(1) == 0)
    last = (pl.program_id(0) == pl.num_programs(0) - 1) & (
        pl.program_id(1) == pl.num_programs(1) - 1)

    @pl.when(first)
    def _():
        g_ref[...] = jnp.zeros_like(g_ref)

    block = fib_ref[:, 0, 0]
    block = block.reshape(block.shape[0] * block.shape[1], block.shape[2])
    half = block.shape[0] // 2
    for a, b in ((0, 0), (0, 1), (1, 1)):
        g_ref[a * half : (a + 1) * half, b * half : (b + 1) * half] += lax.dot_general(
            block[a * half : (a + 1) * half], block[b * half : (b + 1) * half],
            (((1,), (1,)), ((), ())), precision=lax.Precision.HIGH,
            preferred_element_type=jnp.float32)

    @pl.when(last)
    def _():
        g_ref[half:, :half] = g_ref[:half, half:].T


def gram_z_pallas(fib):
    blocks, ys, species, z_local, xs = fib.shape
    size = blocks * z_local
    return pl.pallas_call(
        _gram_z_kernel,
        grid=(ys, species),
        in_specs=[pl.BlockSpec((blocks, 1, 1, z_local, xs), lambda y, s: (0, y, s, 0, 0))],
        out_specs=pl.BlockSpec((size, size), lambda y, s: (0, 0)),
        out_shape=jax.ShapeDtypeStruct((size, size), jnp.float32),
    )(fib)


def _gram_y_kernel(y_local, m_ref, g_ref):
    count = m_ref.shape[0]
    width = m_ref.shape[2] // y_local
    parts = [m_ref[:, 0, a * width : (a + 1) * width] for a in range(y_local)]
    for a in range(y_local):
        for b in range(a, y_local):
            g_ref[a * count : (a + 1) * count, b * count : (b + 1) * count] = lax.dot_general(
                parts[a], parts[b], (((1,), (1,)), ((), ())),
                precision=lax.Precision.HIGH, preferred_element_type=jnp.float32)
    for a in range(y_local):
        for b in range(a):
            g_ref[a * count : (a + 1) * count, b * count : (b + 1) * count] = (
                g_ref[b * count : (b + 1) * count, a * count : (a + 1) * count].T)


def gram_y_pallas(mixed, y_local):
    size = mixed.shape[0] * y_local
    return pl.pallas_call(
        functools.partial(_gram_y_kernel, y_local),
        out_shape=jax.ShapeDtypeStruct((size, size), jnp.float32),
        in_specs=[pl.BlockSpec(memory_space=pltpu.VMEM)],
        out_specs=pl.BlockSpec(memory_space=pltpu.VMEM),
    )(mixed)


def _core_kernel(y_local, m_ref, b_ref, out_ref):
    count = m_ref.shape[0]
    width = m_ref.shape[2] // y_local
    total = None
    for a in range(y_local):
        term = jnp.dot(b_ref[:, a * count : (a + 1) * count], m_ref[:, 0, a * width : (a + 1) * width],
                       precision=lax.Precision.HIGH, preferred_element_type=jnp.float32)
        total = term if total is None else total + term
    out_ref[...] = total


def core_pallas(mixed, basis_perm, y_local):
    rank = basis_perm.shape[1]
    width = mixed.shape[2] // y_local
    return pl.pallas_call(
        functools.partial(_core_kernel, y_local),
        out_shape=jax.ShapeDtypeStruct((rank, width), jnp.float32),
        in_specs=[pl.BlockSpec(memory_space=pltpu.VMEM)] * 2,
        out_specs=pl.BlockSpec(memory_space=pltpu.VMEM),
    )(mixed, basis_perm.T)


def leaf_basis(gram_part, basis_now):
    gram_total = sum_over_mesh(gram_part)
    return basis_pallas(gram_total, basis_now, ITERS)


def body(species_field):
    count_gz = lax.axis_size("gz")
    count_gy = lax.axis_size("gy")
    count = count_gz * count_gy
    fibres = lax.all_to_all(species_field, "gz", split_axis=2, concat_axis=1, tiled=True)
    species, _, y_local, x_size = fibres.shape
    fib5 = fibres.reshape(species, count_gz, -1, y_local, x_size)
    fib5 = jnp.transpose(fib5, (1, 3, 0, 2, 4))
    gram_z = gram_z_pallas(fib5)
    basis_z = leaf_basis(gram_z, start_table(GRID, RANK))
    x_part = x_size // count
    send = reduce_send(fib5, basis_z, count)
    mixed = lax.all_to_all(send, ("gz", "gy"), 0, 0, tiled=True)
    gram_y = gram_y_pallas(mixed, y_local)
    start_y = start_table(GRID, RANK).reshape(count_gy, count_gz, y_local, RANK)
    start_y = jnp.transpose(start_y, (2, 1, 0, 3)).reshape(GRID, RANK)
    basis_perm = leaf_basis(gram_y, start_y)
    core_t = core_pallas(mixed, basis_perm, y_local)
    core_tensor = core_t.reshape(RANK, x_part, species, RANK)
    core_tensor = jnp.transpose(core_tensor, (2, 1, 3, 0)).reshape(species, x_part, RANK * RANK)
    basis_y = basis_perm.reshape(y_local, count_gz, count_gy, RANK)
    basis_y = jnp.transpose(basis_y, (2, 1, 0, 3)).reshape(GRID, RANK)
    return (core_tensor, basis_z, basis_y)


def solution(mesh):
    in_specs = (P(None, "gz", "gy", None),)
    out_specs = (P(None, ("gz", "gy"), None), P(), P())
    return jax.shard_map(body, mesh=mesh, in_specs=in_specs, out_specs=out_specs, check_vma=False)
```

```python
import math

import jax
import jax.numpy as jnp
from jax import lax
from jax.experimental import pallas as pl
from jax.experimental.pallas import tpu as pltpu
from jax.sharding import PartitionSpec as P
import functools

GRID = 512
RANK = 64
ITERS = 4


def start_table(order, width):
    row_index = jnp.arange(order).astype(jnp.float32)
    col_index = jnp.arange(width).astype(jnp.float32)
    return jnp.cos(math.pi * (row_index[:, None] + 0.5) * col_index[None, :] / order)


def solve_factor(product, inner_gram):
    factor = jnp.linalg.cholesky(inner_gram)
    return lax.linalg.triangular_solve(
        factor, product, left_side=False, lower=True, transpose_a=True
    )


def inner_products(left, right):
    return lax.dot_general(left, right, (((0,), (0,)), ((), ())), precision=lax.Precision.HIGHEST)


def mode_products(left, right, mode):
    others = tuple((d for d in range(4) if d != mode))
    return lax.dot_general(
        left, right, ((others, others), ((), ())), precision=lax.Precision.HIGH
    )


def sum_over_mesh(gram):
    axes = ("gz", "gy")
    count = lax.axis_size("gz") * lax.axis_size("gy")
    rows = gram.shape[0]
    if gram.ndim == 2:
        gram = gram.reshape(count, rows // count, rows)
    else:
        rows = gram.shape[2]
    parts = lax.all_to_all(gram, axes, 0, 0, tiled=True)
    mine = parts.sum(0)
    tiled = jnp.broadcast_to(mine[None], (count,) + mine.shape)
    return lax.all_to_all(tiled, axes, 0, 0, tiled=True)


def _eliminate(c):
    n = c.shape[0]
    row = lax.broadcasted_iota(jnp.int32, (n, n), 0)
    lane = lax.broadcasted_iota(jnp.int32, (n, n), 1)
    row_col = row[:, :1]
    right = jnp.where(row == lane, 1.0, 0.0)
    diag = jnp.sum(jnp.where(row == lane, c, 0.0), axis=1, keepdims=True)

    def step(j, carry):
        left, right, diag = carry
        at_row = row == j
        row_l = jnp.sum(jnp.where(at_row, left, 0.0), axis=0, keepdims=True)
        row_r = jnp.sum(jnp.where(at_row, right, 0.0), axis=0, keepdims=True)
        col = jnp.sum(jnp.where(lane == j, left, 0.0), axis=1, keepdims=True)
        pivot = jnp.sum(jnp.where(row_col == j, diag, 0.0), axis=0, keepdims=True)
        factor = jnp.where(row_col > j, col / pivot, 0.0)
        return (left - factor * row_l, right - factor * row_r, diag - factor * col)

    _, right, diag = lax.fori_loop(0, n, step, (c, right, diag), unroll=64)
    return right / jnp.sqrt(diag)


def _basis_kernel(iters, g_ref, q_ref, out_ref):
    gram = g_ref[...]
    gram = gram.reshape(gram.shape[0] * gram.shape[1], gram.shape[2])
    basis_t = q_ref[...]
    for _ in range(iters):
        product_t = jnp.dot(basis_t, gram, precision=lax.Precision.HIGH, preferred_element_type=jnp.float32)
        inner = lax.dot_general(product_t, product_t, (((1,), (1,)), ((), ())),
                                precision=lax.Precision.HIGH, preferred_element_type=jnp.float32)
        basis_t = jnp.dot(_eliminate(inner), product_t, precision=lax.Precision.HIGH,
                          preferred_element_type=jnp.float32)
    out_ref[...] = basis_t


def basis_pallas(gram, start, iters=4):
    size, n = start.shape
    out = pl.pallas_call(
        functools.partial(_basis_kernel, iters),
        out_shape=jax.ShapeDtypeStruct((n, size), jnp.float32),
        in_specs=[pl.BlockSpec(memory_space=pltpu.VMEM)] * 2,
        out_specs=pl.BlockSpec(memory_space=pltpu.VMEM),
    )(gram, start.T)
    return out.T

def _reduce_kernel(count, x_part, rank, fib_ref, bz_ref, out_ref, t_ref):
    y = pl.program_id(0)
    species = fib_ref.shape[2]
    per = 128 // rank
    for s in range(species):
        block = fib_ref[:, 0, s]
        block = block.reshape(block.shape[0] * block.shape[1], block.shape[2])
        t_ref[s // per, :, (s % per) * rank : (s % per + 1) * rank] = jnp.dot(
            bz_ref[...], block,
            precision=lax.Precision.HIGH, preferred_element_type=jnp.float32).T
    width = species * rank
    for xl in range(x_part):
        for h in range(species // per):
            rows = t_ref[h, pl.ds(xl, count, stride=x_part), :]
            col = pl.multiple_of((y * x_part + xl) * width + h * 128, 128)
            out_ref[:, 0, pl.ds(col, 128)] = rows


def reduce_send(fib_ys, basis_z, count):
    blocks, ys, species, z_local, xs = fib_ys.shape
    zs = blocks * z_local
    rank = basis_z.shape[1]
    x_part = xs // count
    return pl.pallas_call(
        functools.partial(_reduce_kernel, count, x_part, rank),
        grid=(ys,),
        in_specs=[pl.BlockSpec((blocks, 1, species, z_local, xs), lambda y: (0, y, 0, 0, 0)),
                  pl.BlockSpec((rank, zs), lambda y: (0, 0))],
        out_specs=pl.BlockSpec((count, 1, ys * x_part * species * rank), lambda y: (0, 0, 0)),
        out_shape=jax.ShapeDtypeStruct((count, 1, ys * x_part * species * rank), jnp.float32),
        scratch_shapes=[pltpu.VMEM((species * rank // 128, xs, 128), jnp.float32)],
        compiler_params=pltpu.CompilerParams(vmem_limit_bytes=48 * 1024 * 1024),
    )(fib_ys, basis_z.T)


def _gram_z_kernel(fib_ref, g_ref):
    first = (pl.program_id(0) == 0) & (pl.program_id(1) == 0)
    last = (pl.program_id(0) == pl.num_programs(0) - 1) & (
        pl.program_id(1) == pl.num_programs(1) - 1)

    @pl.when(first)
    def _():
        g_ref[...] = jnp.zeros_like(g_ref)

    block = fib_ref[:, 0, 0]
    block = block.reshape(block.shape[0] * block.shape[1], block.shape[2])
    half = block.shape[0] // 2
    for a, b in ((0, 0), (0, 1), (1, 1)):
        g_ref[a * half : (a + 1) * half, b * half : (b + 1) * half] += lax.dot_general(
            block[a * half : (a + 1) * half], block[b * half : (b + 1) * half],
            (((1,), (1,)), ((), ())), precision=lax.Precision.HIGH,
            preferred_element_type=jnp.float32)

    @pl.when(last)
    def _():
        g_ref[half:, :half] = g_ref[:half, half:].T


def gram_z_pallas(fib):
    blocks, ys, species, z_local, xs = fib.shape
    size = blocks * z_local
    return pl.pallas_call(
        _gram_z_kernel,
        grid=(ys, species),
        in_specs=[pl.BlockSpec((blocks, 1, 1, z_local, xs), lambda y, s: (0, y, s, 0, 0))],
        out_specs=pl.BlockSpec((size, size), lambda y, s: (0, 0)),
        out_shape=jax.ShapeDtypeStruct((size, size), jnp.float32),
    )(fib)


def _gram_y_kernel(y_local, m_ref, g_ref):
    count = m_ref.shape[0]
    width = m_ref.shape[2] // y_local
    rows = count // y_local
    parts = [m_ref[:, 0, a * width : (a + 1) * width] for a in range(y_local)]
    blocks = {}
    for a in range(y_local):
        for b in range(a, y_local):
            blocks[a, b] = lax.dot_general(
                parts[a], parts[b], (((1,), (1,)), ((), ())),
                precision=lax.Precision.HIGH, preferred_element_type=jnp.float32)
    for a in range(y_local):
        for b in range(a):
            blocks[a, b] = blocks[b, a].T
    for a in range(y_local):
        g_ref[a * rows : (a + 1) * rows] = jnp.concatenate(
            [blocks[a, b] for b in range(y_local)], axis=1).reshape(rows, y_local, -1)


def gram_y_pallas(mixed, y_local):
    count = mixed.shape[0]
    size = count * y_local
    return pl.pallas_call(
        functools.partial(_gram_y_kernel, y_local),
        out_shape=jax.ShapeDtypeStruct((count, y_local, size), jnp.float32),
        in_specs=[pl.BlockSpec(memory_space=pltpu.VMEM)],
        out_specs=pl.BlockSpec(memory_space=pltpu.VMEM),
    )(mixed)


def _core_kernel(y_local, m_ref, b_ref, out_ref):
    count = m_ref.shape[0]
    width = m_ref.shape[2] // y_local
    total = None
    for a in range(y_local):
        term = jnp.dot(b_ref[:, a * count : (a + 1) * count], m_ref[:, 0, a * width : (a + 1) * width],
                       precision=lax.Precision.HIGH, preferred_element_type=jnp.float32)
        total = term if total is None else total + term
    out_ref[...] = total


def core_pallas(mixed, basis_perm, y_local):
    rank = basis_perm.shape[1]
    width = mixed.shape[2] // y_local
    return pl.pallas_call(
        functools.partial(_core_kernel, y_local),
        out_shape=jax.ShapeDtypeStruct((rank, width), jnp.float32),
        in_specs=[pl.BlockSpec(memory_space=pltpu.VMEM)] * 2,
        out_specs=pl.BlockSpec(memory_space=pltpu.VMEM),
    )(mixed, basis_perm.T)


def leaf_basis(gram_part, basis_now):
    gram_total = sum_over_mesh(gram_part)
    return basis_pallas(gram_total, basis_now, ITERS)


def body(species_field):
    count_gz = lax.axis_size("gz")
    count_gy = lax.axis_size("gy")
    count = count_gz * count_gy
    fibres = lax.all_to_all(species_field, "gz", split_axis=2, concat_axis=1, tiled=True)
    species, _, y_local, x_size = fibres.shape
    fib5 = fibres.reshape(species, count_gz, -1, y_local, x_size)
    fib5 = jnp.transpose(fib5, (1, 3, 0, 2, 4))
    gram_z = gram_z_pallas(fib5)
    basis_z = leaf_basis(gram_z, start_table(GRID, RANK))
    x_part = x_size // count
    send = reduce_send(fib5, basis_z, count)
    mixed = lax.all_to_all(send, ("gz", "gy"), 0, 0, tiled=True)
    gram_y = gram_y_pallas(mixed, y_local)
    start_y = start_table(GRID, RANK).reshape(count_gy, count_gz, y_local, RANK)
    start_y = jnp.transpose(start_y, (2, 1, 0, 3)).reshape(GRID, RANK)
    basis_perm = leaf_basis(gram_y, start_y)
    core_t = core_pallas(mixed, basis_perm, y_local)
    core_tensor = core_t.reshape(RANK, x_part, species, RANK)
    core_tensor = jnp.transpose(core_tensor, (2, 1, 3, 0)).reshape(species, x_part, RANK * RANK)
    basis_y = basis_perm.reshape(y_local, count_gz, count_gy, RANK)
    basis_y = jnp.transpose(basis_y, (2, 1, 0, 3)).reshape(GRID, RANK)
    return (core_tensor, basis_z, basis_y)


def solution(mesh):
    in_specs = (P(None, "gz", "gy", None),)
    out_specs = (P(None, ("gz", "gy"), None), P(), P())
    return jax.shard_map(body, mesh=mesh, in_specs=in_specs, out_specs=out_specs, check_vma=False)
```
